256 devices in a mesh: energy: 4 (over z_hi, core), atom: 64 (over z_lo, x, y).
Axes of the slice: x: 4, y: 4, z: 8 (z_hi: 2, z_lo: 4; z = z_hi * 4 + z_lo), core: 2. Of those that a mesh axis runs over, the one named last changes fastest.
Arguments:
- green: bfloat16 [256, 2, 12, 12, 512], P('atom', None, None, None, 'energy'), may hold values from -6 to 6
- coupling: bfloat16 [256, 10368], P('atom'), may hold values from -0.375 to 0.375
- neighbours: int32 [256, 24], P('atom'), may hold values from 0 to 255, as said below
- shifts: int32 [16], replicated, may hold values from 1 to 64, as said below
- weights: float32 [16], replicated, may hold values from 0.1 to 1
Outputs:
- self_energy: bfloat16 [256, 2, 12, 12, 512], P('atom', None, None, None, 'energy')
The draws below stay inside these ranges and needn't reach their ends.
Inputs may be any that keep to these rules, and one draw needn't show every extreme that they name: `neighbours`: of the 24 x 4 entries in the rows of one device's atoms, exactly 12 name atoms held by other devices, at most 2 of them atoms of any one device, and in every draw some device's entries reach 2 for some other device; the other remote entries are spread evenly over the remaining devices. `shifts`: one of them equals 64.
All inputs are finite; a program needn't handle non-finite values.
Results may differ from the reference program's by a relative error of at most 0.012.
Values may be sent and summed in bfloat16 or wider, within the bound.
A program may use at most 128 MiB of HBM per device.

```python
import math
import jax
import jax.numpy as jnp
from jax import lax

ORB = 12
NBR = 24
DIRS = 3
NQ = 16
MAXS = 64
CAP = 2
ATOM_DEV = 4
ATOMS = 256
NE = 512
REMOTE = 12
N_ATOM = 64


def draw_neighbours(key, part):
    slots = NBR * ATOM_DEV

    def one_device(device_key, device):
        key_perm, key_row, key_mix = jax.random.split(device_key, 3)
        others = (device + 1 + jax.random.permutation(key_perm, N_ATOM - 1)) % N_ATOM
        position = jnp.arange(slots)
        beyond = position - (slots - REMOTE) - CAP
        spread = others[1 + jnp.maximum(beyond, 0) % (N_ATOM - 2)]
        holder = jnp.where(position < slots - REMOTE, device, jnp.where(beyond < 0, others[0], spread))
        row_in = jax.random.randint(key_row, (slots,), 0, ATOM_DEV)
        atom_ids = holder * ATOM_DEV + row_in
        shuffle = jax.random.permutation(key_mix, slots)
        return atom_ids[shuffle].reshape(ATOM_DEV, NBR)
    device_keys = jax.random.split(jax.random.fold_in(key, 11), N_ATOM)
    drawn = jax.vmap(one_device)(device_keys, jnp.arange(N_ATOM))
    return drawn.reshape(ATOMS, NBR).astype(jnp.int32)


def draw_shifts(key, part):
    drawn = jax.random.randint(jax.random.fold_in(key, 23), (NQ,), 1, MAXS + 1)
    return drawn.at[0].set(MAXS).astype(jnp.int32)


def block_scale(own_key, extent, cuts, smallest, largest):
    loudness = 1.0
    for dim, shards_of in cuts:
        draws = jax.random.uniform(jax.random.fold_in(jax.random.fold_in(own_key, 6), dim), (shards_of,), jnp.float32, smallest / len(cuts), largest / len(cuts))
        loudness = loudness * jnp.repeat(jnp.exp(draws), extent[dim] // shards_of).reshape((-1,) + (1,) * (len(extent) - 1 - dim))
    return loudness


def normal_values(own_key, shape, scale, reach, shards=(), held_as=jnp.bfloat16):
    array = jax.random.normal(own_key, shape, jnp.float32) * scale
    if len(shards) > 0:
        array = block_scale(own_key, shape, shards, -0.22, 0.18) * array
    return jnp.clip(array, min=-reach, max=reach).astype(held_as)


def setup_inputs(seed: int = 0) -> dict:
    arg_keys = jax.random.split(jax.random.key(seed), 6)
    return {
        "green": normal_values(arg_keys[0], (ATOMS, 2, ORB, ORB, NE), 1.0, 6.0, ((0, 64), (4, 4))),
        "coupling": normal_values(arg_keys[1], (ATOMS, NBR * DIRS * ORB * ORB), (ORB * NBR) ** -0.5, 0.375, ((0, 64),)),
        "neighbours": draw_neighbours(jax.random.fold_in(arg_keys[5], 71), 0),
        "shifts": draw_shifts(jax.random.fold_in(arg_keys[5], 71), 0),
        "weights": jnp.clip(jnp.exp(jax.random.uniform(arg_keys[4], (NQ,), jnp.float32, math.log(0.1), math.log(1.0))), 0.1, 1.0),
    }


def convolve(blocks, shifts, weights, span_out):
    def add_term(term_index, running):
        window = lax.dynamic_slice_in_dim(blocks, shifts[term_index], span_out, blocks.ndim - 1)
        return running + weights[term_index] * window.astype(jnp.float32)
    zeroed = jnp.zeros(blocks.shape[:-1] + (span_out,), jnp.float32)
    return lax.fori_loop(0, shifts.shape[0], add_term, zeroed).astype(jnp.bfloat16)


def reference(green, coupling, neighbours, shifts, weights):
    atom_count = green.shape[0]
    energies = green.shape[-1]
    padded = jnp.concatenate([green, jnp.zeros(green.shape[:-1] + (MAXS,), green.dtype)], axis=4)
    convolved = convolve(padded, shifts, weights, energies)
    matrices = coupling.reshape(atom_count, NBR, DIRS, ORB, ORB)

    def one_atom(packed):
        matrix = packed[0].astype(jnp.float32)
        blocks = convolved[packed[1]].astype(jnp.float32)
        products = jnp.einsum("kdab,kpbce->kdpace", matrix, blocks).astype(jnp.bfloat16)
        summed = jnp.einsum("kdpace,kdfc->pafe", products.astype(jnp.float32), matrix)
        return summed.astype(jnp.bfloat16)

    return lax.map(one_atom, (matrices, neighbours))
```

```python
import functools

import jax
import jax.numpy as jnp
from jax import lax
from jax.experimental import pallas as pl
from jax.experimental.pallas import tpu as pltpu
from jax.sharding import PartitionSpec as P

ORB = 12
NBR = 24
DIRS = 3
NQ = 16
MAXS = 64
ATOMS = 4
REMOTE = 12
SPAN = 128
BLK = ORB * ORB
PADB = ORB * 16
ENTRIES = ATOMS * NBR
TERMS = ATOMS * ATOMS + REMOTE
F32 = jnp.float32
BF16 = jnp.bfloat16


def dot(a, b):
    return jnp.dot(a, b, preferred_element_type=F32)


def conv_kernel(shifts, weights, green, halo, out, wide):
    lag = lax.broadcasted_iota(jnp.int32, (SPAN + MAXS, SPAN), 0) - lax.broadcasted_iota(
        jnp.int32, (SPAN + MAXS, SPAN), 1
    )
    band = jnp.zeros((SPAN + MAXS, SPAN), F32)
    for q in range(NQ):
        band = band + jnp.where(lag == shifts[q], weights[q], 0.0)
    high = band.astype(BF16)
    low = (band - high.astype(F32)).astype(BF16)
    mine, behind = green[...], halo[...]
    wide[...] = (dot(mine, high[:SPAN]) + dot(mine, low[:SPAN])) + (
        dot(behind, high[SPAN:]) + dot(behind, low[SPAN:])
    )
    for part in range(2):
        out[part] = wide[pl.ds(part, ATOMS * BLK, stride=2), :].astype(BF16)


def convolve(green, halo, shifts, weights):
    smem = pl.BlockSpec(memory_space=pltpu.SMEM)
    vmem = pl.BlockSpec(memory_space=pltpu.VMEM)
    return pl.pallas_call(
        conv_kernel,
        out_shape=jax.ShapeDtypeStruct((2, ATOMS * BLK, SPAN), BF16),
        in_specs=[smem, smem, vmem, vmem],
        out_specs=vmem,
        scratch_shapes=[pltpu.VMEM((2 * ATOMS * BLK, SPAN), F32)],
        name="convolve",
    )(shifts, weights, green, halo)


def couple_kernel(slot, term_atom, owner, row, mats, local, everyone, out, r1, r2, m, got, sig, wide, sems):
    copies = []
    for t in range(REMOTE):
        for part in range(2):
            copies.append(
                pltpu.make_async_copy(
                    everyone.at[owner[t], part, pl.ds(pl.multiple_of(row[t] * BLK, BLK), BLK)],
                    got.at[part, pl.ds(t * BLK, BLK)],
                    sems.at[t, part],
                )
            )
    for c in copies:
        c.start()
    x = mats[...]
    kd = x.shape[0]
    source = lax.broadcasted_iota(jnp.int32, (BLK, 2 * SPAN), 0)
    lane = lax.broadcasted_iota(jnp.int32, (BLK, 2 * SPAN), 1)
    group = (lane * 43691) >> 19
    inner = lane - ORB * group
    group = jnp.where(lane < BLK, group, -BLK)
    inner = jnp.where(lane < BLK, inner, -BLK)
    r2[...] = jnp.zeros_like(r2)
    for i in range(ORB):
        spread = dot(x, (source == ORB * i + group).astype(F32).astype(BF16))
        tiled = dot(x, (source == ORB * i + inner).astype(F32).astype(BF16))
        for h in range(2):
            r1.at[h][pl.ds(i, kd, stride=16), :] = spread[:, SPAN * h : SPAN * (h + 1)]
            r2.at[h][pl.ds(i, kd, stride=16), :] = tiled[:, SPAN * h : SPAN * (h + 1)]
    m[...] = jnp.zeros_like(m)

    @pl.loop(0, ENTRIES)
    def _(e):
        base = pl.multiple_of(e * (DIRS * 16), 16)
        at = slot[e]
        for h in range(2):
            right = [r2[h, pl.ds(base + 16 * d, 16), :] for d in range(DIRS)]
            for i in range(ORB):
                total = None
                for d in range(DIRS):
                    left = jnp.broadcast_to(r1[h, pl.ds(base + 16 * d + i, 1), :], (16, SPAN))
                    term = left * right[d]
                    total = term if total is None else total + term
                m[at, pl.ds(16 * i, 16), pl.ds(SPAN * h, SPAN)] += total

    for a in range(ATOMS):
        for part in range(2):
            acc = jnp.zeros((PADB, SPAN), F32)
            for n in range(ATOMS):
                acc = acc + dot(m[a * ATOMS + n][:, :BLK].astype(BF16), local[part, pl.ds(n * BLK, BLK), :])
            sig[part, a] = acc
    for c in copies:
        c.wait()

    @pl.loop(0, REMOTE)
    def _(t):
        k = m[ATOMS * ATOMS + t][:, :BLK].astype(BF16)
        a = term_atom[t]
        at = pl.multiple_of(t * BLK, BLK)
        for part in range(2):
            sig[part, a] += dot(k, got[part, pl.ds(at, BLK), :])

    for a in range(ATOMS):
        for part in range(2):
            for i in range(ORB):
                wide[pl.ds(a * 2 * BLK + i * 2 * ORB + part, ORB, stride=2), :] = sig[
                    part, a, pl.ds(16 * i, ORB), :
                ]
    out[...] = wide[...].astype(BF16)


def couple(slot, term_atom, owner, row, mats, local, everyone):
    smem = pl.BlockSpec(memory_space=pltpu.SMEM)
    vmem = pl.BlockSpec(memory_space=pltpu.VMEM)
    kd = ENTRIES * DIRS
    return pl.pallas_call(
        couple_kernel,
        out_shape=jax.ShapeDtypeStruct((2 * ATOMS * BLK, SPAN), BF16),
        in_specs=[smem, smem, smem, smem, vmem, vmem, pl.BlockSpec(memory_space=pl.ANY)],
        out_specs=vmem,
        scratch_shapes=[
            pltpu.VMEM((2, kd * 16, SPAN), F32),
            pltpu.VMEM((2, kd * 16, SPAN), F32),
            pltpu.VMEM((TERMS, PADB, 2 * SPAN), F32),
            pltpu.VMEM((2, REMOTE * BLK, SPAN), BF16),
            pltpu.VMEM((2, ATOMS, PADB, SPAN), F32),
            pltpu.VMEM((2 * ATOMS * BLK, SPAN), F32),
            pltpu.SemaphoreType.DMA((REMOTE, 2)),
        ],
        compiler_params=pltpu.CompilerParams(vmem_limit_bytes=48 * 1024 * 1024),
        name="couple",
    )(slot, term_atom, owner, row, mats, local, everyone)


def from_behind(value, axis, by):
    peers = lax.axis_size(axis)
    pairs = [(i, i + by) for i in range(peers) if 0 <= i + by < peers]
    return lax.ppermute(value, axis, pairs)


def plan(neighbours):
    me = lax.axis_index("atom")
    ids = neighbours.reshape(-1)
    owner, row = ids // ATOMS, ids % ATOMS
    remote = owner != me
    entry = jnp.arange(ENTRIES, dtype=jnp.int32)
    before = (entry[:, None] <= entry[None, :]) & remote[:, None]
    rank = jnp.sum(before.astype(jnp.int32), axis=0) - 1
    slot = jnp.where(remote, ATOMS * ATOMS + rank, (entry // NBR) * ATOMS + row)
    pick = (rank[None, :] == jnp.arange(REMOTE, dtype=jnp.int32)[:, None]) & remote[None, :]
    packed = jnp.sum(jnp.where(pick, (ids * ATOMS + entry // NBR)[None, :], 0), axis=1)
    return slot, packed % ATOMS, packed // (ATOMS * ATOMS), (packed // ATOMS) % ATOMS


def rows_of(blocks):
    return blocks.transpose(0, 2, 3, 1, 4).reshape(2 * ATOMS * BLK, blocks.shape[-1])


def on_device(green, coupling, neighbours, shifts, weights):
    halo = from_behind(green[..., :MAXS], "energy", -1)
    local = convolve(rows_of(green), rows_of(halo), shifts, weights)
    everyone = lax.all_gather(local, "atom")
    slot, term_atom, owner, row = plan(neighbours)
    mats = coupling.reshape(ENTRIES * DIRS, BLK)
    out = couple(slot, term_atom, owner, row, mats, local, everyone)
    return out.reshape(ATOMS, ORB, ORB, 2, SPAN).transpose(0, 3, 1, 2, 4)


def solution(mesh):
    placed = (P("atom", None, None, None, "energy"), P("atom", None), P("atom", None), P(), P())
    return jax.shard_map(
        on_device,
        mesh=mesh,
        in_specs=placed,
        out_specs=P("atom", None, None, None, "energy"),
        check_vma=False,
    )
```

```python
import functools

import jax
import jax.numpy as jnp
from jax import lax
from jax.experimental import pallas as pl
from jax.experimental.pallas import tpu as pltpu
from jax.sharding import PartitionSpec as P

ORB = 12
NBR = 24
DIRS = 3
NQ = 16
MAXS = 64
ATOMS = 4
REMOTE = 12
SPAN = 128
BLK = ORB * ORB
PADB = ORB * 16
ENTRIES = ATOMS * NBR
TERMS = ATOMS * ATOMS + REMOTE
F32 = jnp.float32
BF16 = jnp.bfloat16


def dot(a, b):
    return jnp.dot(a, b, preferred_element_type=F32)


def conv_kernel(shifts, weights, green, halo, out, wide):
    lag = lax.broadcasted_iota(jnp.int32, (SPAN + MAXS, SPAN), 0) - lax.broadcasted_iota(
        jnp.int32, (SPAN + MAXS, SPAN), 1
    )
    band = jnp.zeros((SPAN + MAXS, SPAN), F32)
    for q in range(NQ):
        band = band + jnp.where(lag == shifts[q], weights[q], 0.0)
    high = band.astype(BF16)
    low = (band - high.astype(F32)).astype(BF16)
    mine, behind = green[...], halo[...]
    wide[...] = (dot(mine, high[:SPAN]) + dot(mine, low[:SPAN])) + (
        dot(behind, high[SPAN:]) + dot(behind, low[SPAN:])
    )
    for part in range(2):
        out[part] = wide[pl.ds(part, ATOMS * BLK, stride=2), :].astype(BF16)


def convolve(green, halo, shifts, weights):
    smem = pl.BlockSpec(memory_space=pltpu.SMEM)
    vmem = pl.BlockSpec(memory_space=pltpu.VMEM)
    return pl.pallas_call(
        conv_kernel,
        out_shape=jax.ShapeDtypeStruct((2, ATOMS * BLK, SPAN), BF16),
        in_specs=[smem, smem, vmem, vmem],
        out_specs=vmem,
        scratch_shapes=[pltpu.VMEM((2 * ATOMS * BLK, SPAN), F32)],
        name="convolve",
    )(shifts, weights, green, halo)


def couple_kernel(slot, term_atom, mats, local, got, out, r1, r2, m, sig, wide):
    x = mats[...]
    kd = x.shape[0]
    source = lax.broadcasted_iota(jnp.int32, (BLK, 2 * SPAN), 0)
    lane = lax.broadcasted_iota(jnp.int32, (BLK, 2 * SPAN), 1)
    group = (lane * 43691) >> 19
    inner = lane - ORB * group
    group = jnp.where(lane < BLK, group, -BLK)
    inner = jnp.where(lane < BLK, inner, -BLK)
    r2[...] = jnp.zeros_like(r2)
    for i in range(ORB):
        spread = dot(x, (source == ORB * i + group).astype(F32).astype(BF16))
        tiled = dot(x, (source == ORB * i + inner).astype(F32).astype(BF16))
        for h in range(2):
            r1.at[h][pl.ds(i, kd, stride=16), :] = spread[:, SPAN * h : SPAN * (h + 1)]
            r2.at[h][pl.ds(i, kd, stride=16), :] = tiled[:, SPAN * h : SPAN * (h + 1)]
    m[...] = jnp.zeros_like(m)

    @pl.loop(0, ENTRIES)
    def _(e):
        base = pl.multiple_of(e * (DIRS * 16), 16)
        at = slot[e]
        for h in range(2):
            right = [r2[h, pl.ds(base + 16 * d, 16), :] for d in range(DIRS)]
            for i in range(ORB):
                total = None
                for d in range(DIRS):
                    left = jnp.broadcast_to(r1[h, pl.ds(base + 16 * d + i, 1), :], (16, SPAN))
                    term = left * right[d]
                    total = term if total is None else total + term
                m[at, pl.ds(16 * i, 16), pl.ds(SPAN * h, SPAN)] += total

    for a in range(ATOMS):
        for part in range(2):
            acc = jnp.zeros((PADB, SPAN), F32)
            for n in range(ATOMS):
                acc = acc + dot(m[a * ATOMS + n][:, :BLK].astype(BF16), local[part, pl.ds(n * BLK, BLK), :])
            sig[part, a] = acc
    @pl.loop(0, REMOTE)
    def _(t):
        k = m[ATOMS * ATOMS + t][:, :BLK].astype(BF16)
        a = term_atom[t]
        at = pl.multiple_of(t * BLK, BLK)
        for part in range(2):
            sig[part, a] += dot(k, got[part, pl.ds(at, BLK), :])

    for a in range(ATOMS):
        for part in range(2):
            for i in range(ORB):
                wide[pl.ds(a * 2 * BLK + i * 2 * ORB + part, ORB, stride=2), :] = sig[
                    part, a, pl.ds(16 * i, ORB), :
                ]
    out[...] = wide[...].astype(BF16)


def couple(slot, term_atom, mats, local, got):
    smem = pl.BlockSpec(memory_space=pltpu.SMEM)
    vmem = pl.BlockSpec(memory_space=pltpu.VMEM)
    kd = ENTRIES * DIRS
    return pl.pallas_call(
        couple_kernel,
        out_shape=jax.ShapeDtypeStruct((2 * ATOMS * BLK, SPAN), BF16),
        in_specs=[smem, smem, vmem, vmem, vmem],
        out_specs=vmem,
        scratch_shapes=[
            pltpu.VMEM((2, kd * 16, SPAN), F32),
            pltpu.VMEM((2, kd * 16, SPAN), F32),
            pltpu.VMEM((TERMS, PADB, 2 * SPAN), F32),
            pltpu.VMEM((2, ATOMS, PADB, SPAN), F32),
            pltpu.VMEM((2 * ATOMS * BLK, SPAN), F32),
        ],
        compiler_params=pltpu.CompilerParams(vmem_limit_bytes=48 * 1024 * 1024),
        name="couple",
    )(slot, term_atom, mats, local, got)


def exchange_kernel(codes, local, got, buf, rec, out, mid, idv, ids, barrier_sems, zs, zr, rs, rr, fs, fr, cs, cr):
    me = lax.axis_index("atom")
    z, x, y = me // 16, (me // 4) % 4, me % 4

    def device(dz, dx, dy):
        return {"atom": (z + dz) * 16 + ((x + dx) % 4) * 4 + (y + dy) % 4}

    def remote(src, dst, send, recv, to):
        return pltpu.make_async_remote_copy(
            src_ref=src,
            dst_ref=dst,
            send_sem=send,
            recv_sem=recv,
            device_id=to,
            device_id_type=pl.DeviceIdType.MESH,
        )

    ring = (x, y)
    ring_to = (lambda d: device(0, d, 0), lambda d: device(0, 0, d))
    last = (y, x)
    last_to = (ring_to[1], ring_to[0])
    down, up = device(-1, 0, 0), device(1, 0, 0)

    barrier = pltpu.get_barrier_semaphore()
    for to in (ring_to[0](1), ring_to[0](-1), ring_to[1](1), ring_to[1](-1)):
        pl.semaphore_signal(barrier, inc=1, device_id=to, device_id_type=pl.DeviceIdType.MESH)

    @pl.when(z > 0)
    def _():
        pl.semaphore_signal(barrier, inc=1, device_id=down, device_id_type=pl.DeviceIdType.MESH)

    @pl.when(z < 3)
    def _():
        pl.semaphore_signal(barrier, inc=1, device_id=up, device_id_type=pl.DeviceIdType.MESH)

    pl.semaphore_wait(barrier, 6 - z // 3 - (3 - z) // 3)

    def place(p, r, s):
        return buf.at[p, pl.ds((r * 4 + s) * 4, 4)]

    mine = [
        pltpu.make_async_copy(local.at[p], place(p, ring[p], z), barrier_sems.at[p]) for p in range(2)
    ]
    for c in mine:
        c.start()

    sent = []
    for p in range(2):
        for i, d in enumerate((1, -1)):
            c = remote(codes, idv.at[p, last[p]], cs.at[p, i], cr.at[p, i], last_to[p](d))
            c.start()
            sent.append(c)
    own_codes = [pltpu.make_async_copy(codes, ids.at[p, last[p]], barrier_sems.at[2 + p]) for p in range(2)]
    for c in own_codes:
        c.start()
    for c in mine:
        c.wait()

    def climb(p, k, s):
        spot = place(p, ring[p], s)
        return remote(spot, spot, zs.at[p, 0, k], zr.at[p, 0, k], up)

    def descend(p, k, s):
        spot = place(p, ring[p], s)
        return remote(spot, spot, zs.at[p, 1, k], zr.at[p, 1, k], down)

    def around(p, i, s):
        spot = place(p, ring[p], s)
        return remote(spot, spot, rs.at[p, i, s], rr.at[p, i, s], ring_to[p](1 - 2 * i))

    def onward(p, i, s):
        spot = place(p, (ring[p] + (3, 1)[i]) % 4, s)
        return remote(spot, spot, rs.at[p, 2, s], rr.at[p, 2, s], ring_to[p](1 - 2 * i))

    def deliver(p, s):
        around(p, 0, s).start()
        around(p, 1, s).start()

    def arrived(p, r, s, i):
        spot = place(p, r, s)
        remote(spot, spot, rs.at[p, i, s], rr.at[p, i, s], ring_to[p](1)).wait_recv()

    def relay(p, s):
        arrived(p, (ring[p] + 3) % 4, s, 0)

        @pl.when(s < 2)
        def _():
            onward(p, 0, s).start()

        arrived(p, (ring[p] + 1) % 4, s, 1)

        @pl.when(s >= 2)
        def _():
            onward(p, 1, s).start()

    for p in range(2):

        @pl.when(z < 3)
        def _():
            climb(p, 0, z).start()

        @pl.when(z > 0)
        def _():
            descend(p, 0, z).start()

        deliver(p, z)

    for p in range(2):
        remote(codes, idv.at[p, (last[p] + 3) % 4], cs.at[p, 0], cr.at[p, 0], last_to[p](-1)).wait_recv()
        c = remote(
            idv.at[p, (last[p] + 3) % 4], idv.at[p, (last[p] + 3) % 4], cs.at[p, 2], cr.at[p, 2], last_to[p](1)
        )
        c.start()
        sent.append(c)

    for k in range(4):
        if k < 3:
            for p in range(2):

                @pl.when(z - 1 - k >= 0)
                def _():
                    s = z - 1 - k
                    spot = place(p, ring[p], s)
                    remote(spot, spot, zs.at[p, 0, k], zr.at[p, 0, k], down).wait_recv()
                    if k < 2:

                        @pl.when(z < 3)
                        def _():
                            climb(p, k + 1, s).start()

                    deliver(p, s)

                @pl.when(z + 1 + k <= 3)
                def _():
                    s = z + 1 + k
                    spot = place(p, ring[p], s)
                    remote(spot, spot, zs.at[p, 1, k], zr.at[p, 1, k], up).wait_recv()
                    if k < 2:

                        @pl.when(z > 0)
                        def _():
                            descend(p, k + 1, s).start()

                    deliver(p, s)

        for p in range(2):
            if k == 0:
                relay(p, z)
            else:

                @pl.when(z - k >= 0)
                def _():
                    relay(p, z - k)

                @pl.when(z + k <= 3)
                def _():
                    relay(p, z + k)

    for c in own_codes:
        c.wait()
    moved = []
    for p in range(2):
        remote(codes, idv.at[p, (last[p] + 1) % 4], cs.at[p, 1], cr.at[p, 1], last_to[p](1)).wait_recv()
        remote(codes, idv.at[p, (last[p] + 2) % 4], cs.at[p, 2], cr.at[p, 2], last_to[p](1)).wait_recv()
        for j in range(1, 4):
            c = pltpu.make_async_copy(
                idv.at[p, (last[p] + j) % 4], ids.at[p, (last[p] + j) % 4], barrier_sems.at[4 + 3 * p + j - 1]
            )
            c.start()
            moved.append(c)
    for c in moved:
        c.wait()
    for p in range(2):
        for s in range(4):
            arrived(p, (ring[p] + 2) % 4, s, 2)

    def choose(p, i, peer, first, count):
        @pl.loop(0, count)
        def _(t):
            out[p, i, first + t] = buf[p, ids[p, peer, p, (0 if i < 2 else (i - 2) * (REMOTE // 2)) + t]]

    half = REMOTE // 2
    for p in range(2):
        opposite = (last[p] + 2) % 4
        for i in range(2):
            choose(p, 2 + i, opposite, 0, half)
            c = remote(
                out.at[p, 2 + i, pl.ds(0, half)], mid.at[p, i], fs.at[p, 2 + i], fr.at[p, 2 + i], last_to[p](1 - 2 * i)
            )
            c.start()
            sent.append(c)
    for p in range(2):
        for i in range(2):
            choose(p, i, (last[p] + (1, 3)[i]) % 4, 0, REMOTE)
            c = remote(
                out.at[p, i], rec.at[p, pl.ds(last[p] * REMOTE, REMOTE)], fs.at[p, i], fr.at[p, i], last_to[p](1 - 2 * i)
            )
            c.start()
            sent.append(c)
    for p in range(2):
        for i in range(2):
            remote(mid.at[p, i], mid.at[p, i], fs.at[p, 2 + i], fr.at[p, 2 + i], last_to[p](1)).wait_recv()
            c = remote(
                mid.at[p, i],
                rec.at[p, pl.ds(((last[p] + (3, 1)[i]) % 4) * REMOTE + half * i, half)],
                fs.at[p, 4 + i],
                fr.at[p, 4 + i],
                last_to[p](1 - 2 * i),
            )
            c.start()
            sent.append(c)

        @pl.loop(0, REMOTE)
        def _(t):
            rec[p, last[p] * REMOTE + t] = buf[p, ids[p, last[p], p, t]]

    for p in range(2):
        for i in range(2):
            spot = rec.at[p, pl.ds(((last[p] + (3, 1)[i]) % 4) * REMOTE, REMOTE)]
            remote(spot, spot, fs.at[p, i], fr.at[p, i], last_to[p](1)).wait_recv()
            spot = rec.at[p, pl.ds(((last[p] + 2) % 4) * REMOTE + half * i, half)]
            remote(spot, spot, fs.at[p, 4 + i], fr.at[p, 4 + i], last_to[p](1)).wait_recv()
    for p in range(2):

        @pl.loop(0, REMOTE)
        def _(t):
            got[p, t] = rec[p, ids[p, last[p], 2 + p, t] * REMOTE + t]

    for c in sent:
        c.wait_send()
    for p in range(2):
        for k in range(3):

            @pl.when((z < 3) & (z - k >= 0))
            def _():
                climb(p, k, z - k).wait_send()

            @pl.when((z > 0) & (z + k <= 3))
            def _():
                descend(p, k, z + k).wait_send()

        for s in range(4):
            around(p, 0, s).wait_send()
            around(p, 1, s).wait_send()
            onward(p, s // 2, s).wait_send()


def exchange(codes, local):
    vmem = pl.BlockSpec(memory_space=pltpu.VMEM)
    blk = local.shape[-2]
    dma = pltpu.SemaphoreType.DMA
    return pl.pallas_call(
        exchange_kernel,
        out_shape=jax.ShapeDtypeStruct((2, REMOTE, blk, SPAN), BF16),
        in_specs=[vmem, vmem],
        out_specs=vmem,
        scratch_shapes=[
            pltpu.VMEM((2, 64, blk, SPAN), BF16),
            pltpu.VMEM((2, 4 * REMOTE, blk, SPAN), BF16),
            pltpu.VMEM((2, 4, REMOTE, blk, SPAN), BF16),
            pltpu.VMEM((2, 2, REMOTE // 2, blk, SPAN), BF16),
            pltpu.VMEM((2, 4, 8, SPAN), jnp.int32),
            pltpu.SMEM((2, 4, 8, SPAN), jnp.int32),
            dma((10,)),
            dma((2, 2, 3)),
            dma((2, 2, 3)),
            dma((2, 3, 4)),
            dma((2, 3, 4)),
            dma((2, 6)),
            dma((2, 6)),
            dma((2, 3)),
            dma((2, 3)),
        ],
        compiler_params=pltpu.CompilerParams(
            collective_id=0, has_side_effects=True, vmem_limit_bytes=48 * 1024 * 1024
        ),
        name="exchange",
    )(codes, local)


def from_behind(value, axis, by):
    peers = lax.axis_size(axis)
    pairs = [(i, i + by) for i in range(peers) if 0 <= i + by < peers]
    return lax.ppermute(value, axis, pairs)


def plan(neighbours):
    me = lax.axis_index("atom")
    ids = neighbours.reshape(-1)
    owner, row = ids // ATOMS, ids % ATOMS
    remote = owner != me
    entry = jnp.arange(ENTRIES, dtype=jnp.int32)
    before = (entry[:, None] <= entry[None, :]) & remote[:, None]
    rank = jnp.sum(before.astype(jnp.int32), axis=0) - 1
    slot = jnp.where(remote, ATOMS * ATOMS + rank, (entry // NBR) * ATOMS + row)
    pick = (rank[None, :] == jnp.arange(REMOTE, dtype=jnp.int32)[:, None]) & remote[None, :]
    packed = jnp.sum(jnp.where(pick, (ids * ATOMS + entry // NBR)[None, :], 0), axis=1)
    source = packed // ATOMS
    at_row, at_y, at_x, at_z = source % 4, (source // 4) % 4, (source // 16) % 4, source // 64
    lists = jnp.stack([(at_x * 4 + at_z) * 4 + at_row, (at_y * 4 + at_z) * 4 + at_row, at_y, at_x])
    codes = jnp.zeros((8, SPAN), jnp.int32).at[:4, :REMOTE].set(lists)
    return slot, packed % ATOMS, codes


def rows_of(blocks):
    return blocks.transpose(0, 2, 3, 1, 4).reshape(2 * ATOMS * BLK, blocks.shape[-1])


def on_device(green, coupling, neighbours, shifts, weights):
    halo = from_behind(green[..., :MAXS], "energy", -1)
    local = convolve(rows_of(green), rows_of(halo), shifts, weights)
    slot, term_atom, codes = plan(neighbours)
    got = exchange(codes, local.reshape(2, ATOMS, BLK, SPAN))
    mats = coupling.reshape(ENTRIES * DIRS, BLK)
    out = couple(slot, term_atom, mats, local, got.reshape(2, REMOTE * BLK, SPAN))
    return out.reshape(ATOMS, ORB, ORB, 2, SPAN).transpose(0, 3, 1, 2, 4)


def solution(mesh):
    placed = (P("atom", None, None, None, "energy"), P("atom", None), P("atom", None), P(), P())
    return jax.shard_map(
        on_device,
        mesh=mesh,
        in_specs=placed,
        out_specs=P("atom", None, None, None, "energy"),
        check_vma=False,
    )
```

```python
import functools

import jax
import jax.numpy as jnp
from jax import lax
from jax.experimental import pallas as pl
from jax.experimental.pallas import tpu as pltpu
from jax.sharding import PartitionSpec as P

ORB = 12
NBR = 24
DIRS = 3
NQ = 16
MAXS = 64
ATOMS = 4
REMOTE = 12
SPAN = 128
BLK = ORB * ORB
ENTRIES = ATOMS * NBR
F32 = jnp.float32
BF16 = jnp.bfloat16


def dot(a, b):
    return jnp.dot(a, b, preferred_element_type=F32)


def conv_kernel(shifts, weights, green, halo, out, wide):
    lag = lax.broadcasted_iota(jnp.int32, (SPAN + MAXS, SPAN), 0) - lax.broadcasted_iota(
        jnp.int32, (SPAN + MAXS, SPAN), 1
    )
    band = jnp.zeros((SPAN + MAXS, SPAN), F32)
    for q in range(NQ):
        band = band + jnp.where(lag == shifts[q], weights[q], 0.0)
    high = band.astype(BF16)
    low = (band - high.astype(F32)).astype(BF16)
    mine, behind = green[...], halo[...]
    wide[...] = (dot(mine, high[:SPAN]) + dot(mine, low[:SPAN])) + (
        dot(behind, high[SPAN:]) + dot(behind, low[SPAN:])
    )
    for part in range(2):
        out[part] = wide[pl.ds(part, ATOMS * BLK, stride=2), :].astype(BF16)


def convolve(green, halo, shifts, weights):
    smem = pl.BlockSpec(memory_space=pltpu.SMEM)
    vmem = pl.BlockSpec(memory_space=pltpu.VMEM)
    return pl.pallas_call(
        conv_kernel,
        out_shape=jax.ShapeDtypeStruct((2, ATOMS * BLK, SPAN), BF16),
        in_specs=[smem, smem, vmem, vmem],
        out_specs=vmem,
        scratch_shapes=[pltpu.VMEM((2 * ATOMS * BLK, SPAN), F32)],
        name="convolve",
    )(shifts, weights, green, halo)


def spreaders(qs):
    source = lax.broadcasted_iota(jnp.int32, (BLK, 2 * SPAN), 0)
    lane = lax.broadcasted_iota(jnp.int32, (BLK, 2 * SPAN), 1)
    group = (lane * 43691) >> 19
    inner = jnp.where(lane < BLK, lane - ORB * group, -BLK)
    group = jnp.where(lane < BLK, group, -BLK)
    for i in range(ORB):
        qs[i] = (source == ORB * i + group).astype(F32).astype(BF16)
        qs[ORB + i] = (source == ORB * i + inner).astype(F32).astype(BF16)


def expand(x, qs, r1, r2):
    rows = x.shape[0]
    for i in range(ORB):
        r1[i, pl.ds(0, rows), :] = dot(x, qs[i])
        r2[i, pl.ds(0, rows), :] = dot(x, qs[ORB + i])


def products(rows, r1, r2, kt):
    half = ORB // 2

    @pl.loop(0, rows // 8)
    def _(c):
        row = pl.multiple_of(c * 8, 8)
        for h in range(2):
            lanes = pl.ds(SPAN * h, SPAN)
            for g in range(2):
                left = [
                    [r1[half * g + i, pl.ds(rows * d + row, 8), lanes] for d in range(DIRS)] for i in range(half)
                ]
                for f in range(ORB):
                    right = [r2[f, pl.ds(rows * d + row, 8), lanes] for d in range(DIRS)]
                    for i in range(half):
                        total = left[i][0] * right[0] + left[i][1] * right[1] + left[i][2] * right[2]
                        kt[h, pl.ds(((half * g + i) * ORB + f) * rows + row, 8), :] = total


def pick_matrix(kt, first, stride):
    parts = [kt.at[h][pl.ds(first, BLK, stride=stride), :] for h in range(2)]
    return jnp.concatenate(parts, axis=1)[:, :BLK].astype(BF16)


def self_energy_kernel(
    codes,
    key,
    where,
    mats,
    local,
    out,
    buf0,
    buf1,
    rec,
    snd,
    mid,
    idv,
    ids,
    crem,
    crv,
    qs,
    r1,
    r2,
    kt,
    mt,
    kr,
    sst,
    sig,
    wide,
    ls,
    zs,
    zr,
    rs,
    rr,
    fs,
    fr,
    cs,
    cr,
    ps,
    pr,
):
    me = lax.axis_index("atom")
    z, x, y = me // 16, (me // 4) % 4, me % 4
    buf = (buf0, buf1)

    def device(dz, dx, dy):
        return {"atom": (z + dz) * 16 + ((x + dx) % 4) * 4 + (y + dy) % 4}

    def remote(src, dst, send, recv, to):
        return pltpu.make_async_remote_copy(
            src_ref=src,
            dst_ref=dst,
            send_sem=send,
            recv_sem=recv,
            device_id=to,
            device_id_type=pl.DeviceIdType.MESH,
        )

    ring = (x, y)
    ring_to = (lambda d: device(0, d, 0), lambda d: device(0, 0, d))
    last = (y, x)
    last_to = (ring_to[1], ring_to[0])
    down, up = device(-1, 0, 0), device(1, 0, 0)

    barrier = pltpu.get_barrier_semaphore()
    for to in (ring_to[0](1), ring_to[0](-1), ring_to[1](1), ring_to[1](-1)):
        pl.semaphore_signal(barrier, inc=1, device_id=to, device_id_type=pl.DeviceIdType.MESH)

    @pl.when(z > 0)
    def _():
        pl.semaphore_signal(barrier, inc=1, device_id=down, device_id_type=pl.DeviceIdType.MESH)

    @pl.when(z < 3)
    def _():
        pl.semaphore_signal(barrier, inc=1, device_id=up, device_id_type=pl.DeviceIdType.MESH)

    row = lax.broadcasted_iota(jnp.int32, (DIRS * 16, ENTRIES * DIRS), 0)
    choice = (row == jnp.broadcast_to(key[...], row.shape)).astype(F32).astype(BF16)
    crem[...] = dot(choice, mats[...]).astype(BF16)
    pl.semaphore_wait(barrier, 6 - z // 3 - (3 - z) // 3)

    def place(p, r, s):
        return buf[p].at[pl.ds((r * 4 + s) * 4, 4)]

    mine = [pltpu.make_async_copy(local.at[p], place(p, ring[p], z), ls.at[p]) for p in range(2)]
    for c in mine:
        c.start()

    def ask(p, i, src, codes_src, slot, to):
        return [
            remote(codes_src, idv.at[p, slot], cs.at[p, i], cr.at[p, i], to),
            remote(src, crv.at[p, slot], ps.at[p, i], pr.at[p, i], to),
        ]

    sent = []
    for p in range(2):
        for i, d in enumerate((1, -1)):
            for c in ask(p, i, crem, codes, last[p], last_to[p](d)):
                c.start()
                sent.append(c)
    own_codes = [pltpu.make_async_copy(codes, ids.at[p, last[p]], ls.at[2 + p]) for p in range(2)]
    for c in own_codes:
        c.start()
    for c in mine:
        c.wait()

    def climb(p, k, s):
        spot = place(p, ring[p], s)
        return remote(spot, spot, zs.at[p, 0, k], zr.at[p, 0, k], up)

    def descend(p, k, s):
        spot = place(p, ring[p], s)
        return remote(spot, spot, zs.at[p, 1, k], zr.at[p, 1, k], down)

    def around(p, i, s):
        spot = place(p, ring[p], s)
        return remote(spot, spot, rs.at[p, i, s], rr.at[p, i, s], ring_to[p](1 - 2 * i))

    def onward(p, i, s):
        spot = place(p, (ring[p] + (3, 1)[i]) % 4, s)
        return remote(spot, spot, rs.at[p, 2, s], rr.at[p, 2, s], ring_to[p](1 - 2 * i))

    def deliver(p, s):
        around(p, 0, s).start()
        around(p, 1, s).start()

    def arrived(p, r, s, i):
        spot = place(p, r, s)
        remote(spot, spot, rs.at[p, i, s], rr.at[p, i, s], ring_to[p](1)).wait_recv()

    def relay(p, s):
        arrived(p, (ring[p] + 3) % 4, s, 0)

        @pl.when(s < 2)
        def _():
            onward(p, 0, s).start()

        arrived(p, (ring[p] + 1) % 4, s, 1)

        @pl.when(s >= 2)
        def _():
            onward(p, 1, s).start()

    for p in range(2):

        @pl.when(z < 3)
        def _():
            climb(p, 0, z).start()

        @pl.when(z > 0)
        def _():
            descend(p, 0, z).start()

        deliver(p, z)

    def local_products():
        spreaders(qs)
        xs = mats[...]
        kd = ENTRIES * DIRS
        to = lax.broadcasted_iota(jnp.int32, (kd, kd), 0)
        at = lax.broadcasted_iota(jnp.int32, (kd, kd), 1)
        order = jnp.zeros((kd, kd), jnp.bool_)
        for d in range(DIRS):
            order = order | ((to >= ENTRIES * d) & (to < ENTRIES * (d + 1)) & (at == (to - ENTRIES * d) * DIRS + d))
        expand(dot(order.astype(F32).astype(BF16), xs).astype(BF16), qs, r1, r2)
        products(ENTRIES, r1, r2, kt)

    def local_sums():
        to = lax.broadcasted_iota(jnp.int32, (ATOMS * ATOMS, ENTRIES), 0)
        spread = (to == jnp.broadcast_to(where[...], to.shape)).astype(F32).astype(BF16)

        @pl.loop(0, BLK, step=4)
        def _(r):
            for u in range(4):
                at = pl.multiple_of((r + u) * ENTRIES, 8)
                both = jnp.concatenate([kt[h, pl.ds(at, ENTRIES), :] for h in range(2)], axis=1)
                summed = dot(spread, both.astype(BF16))
                for h in range(2):
                    mt[h, pl.ds((r + u) * 16, 16), :] = summed[:, SPAN * h : SPAN * (h + 1)]

    def local_energy():
        for a in range(ATOMS):
            acc = [jnp.zeros((BLK, SPAN), F32)] * 2
            for n in range(ATOMS):
                m = pick_matrix(mt, a * ATOMS + n, 16)
                for p in range(2):
                    acc[p] = acc[p] + dot(m, local[p, n])
            for p in range(2):
                sig[p, a] = acc[p]

    def forward_lists():
        for p in range(2):
            slot = (last[p] + 3) % 4
            for c in ask(p, 0, crem, codes, slot, last_to[p](-1)):
                c.wait_recv()
            for c in ask(p, 2, crv.at[p, slot], idv.at[p, slot], slot, last_to[p](1)):
                c.start()
                sent.append(c)

    def take_lists():
        moved = []
        for p in range(2):
            for i, j in ((1, 1), (2, 2)):
                slot = (last[p] + j) % 4
                for c in ask(p, i, crv.at[p, slot], idv.at[p, slot], slot, last_to[p](1)):
                    c.wait_recv()
            for j in range(1, 4):
                slot = (last[p] + j) % 4
                c = pltpu.make_async_copy(idv.at[p, slot], ids.at[p, slot], ls.at[4 + 3 * p + j - 1])
                c.start()
                moved.append(c)
        for c in own_codes + moved:
            c.wait()

    def remote_products():
        sets = [crem[...]] + [crv[p, (last[p] + j) % 4] for p in range(2) for j in range(1, 4)]
        xs = jnp.concatenate([v[16 * d : 16 * (d + 1)] for d in range(DIRS) for v in sets], axis=0)
        expand(xs, qs, r1, r2)
        products(7 * 16, r1, r2, kt)

    def remote_matrices():
        @pl.loop(0, 7 * REMOTE, step=2)
        def _(e):
            for u in range(2):
                kr[e + u] = pick_matrix(kt, (e + u) // REMOTE * 16 + (e + u) % REMOTE, 7 * 16)

    work = {
        0: [forward_lists, local_products],
        1: [local_sums, local_energy],
        2: [take_lists, remote_products],
        3: [remote_matrices],
    }
    for k in range(4):
        for piece in work[k]:
            piece()
        if k < 3:
            for p in range(2):

                @pl.when(z - 1 - k >= 0)
                def _():
                    s = z - 1 - k
                    spot = place(p, ring[p], s)
                    remote(spot, spot, zs.at[p, 0, k], zr.at[p, 0, k], down).wait_recv()
                    if k < 2:

                        @pl.when(z < 3)
                        def _():
                            climb(p, k + 1, s).start()

                    deliver(p, s)

                @pl.when(z + 1 + k <= 3)
                def _():
                    s = z + 1 + k
                    spot = place(p, ring[p], s)
                    remote(spot, spot, zs.at[p, 1, k], zr.at[p, 1, k], up).wait_recv()
                    if k < 2:

                        @pl.when(z > 0)
                        def _():
                            descend(p, k + 1, s).start()

                    deliver(p, s)

        for p in range(2):
            if k == 0:
                relay(p, z)
            else:

                @pl.when(z - k >= 0)
                def _():
                    relay(p, z - k)

                @pl.when(z + k <= 3)
                def _():
                    relay(p, z + k)

    for p in range(2):
        buf[p][64] = jnp.zeros((BLK, SPAN), BF16)

    def contribution(p, j):
        slot = (last[p] + j) % 4
        q = 0 if j == 0 else 3 * p + j
        running = None
        for t in range(REMOTE):
            source = jnp.where(ids[p, slot, 2 + p, t] == last[p], ids[p, slot, p, t], 64)
            term = dot(kr[q * REMOTE + t], buf[p][source])
            keep = ids[p, slot, 4, t].astype(F32)
            running = term if running is None else keep * running + term
            sst[t] = running
        return [sst[ids[p, slot, 5, a]] * ids[p, slot, 6, a].astype(F32) for a in range(ATOMS)]

    def offer(p, j):
        for a, v in enumerate(contribution(p, j)):
            snd[p, j, a] = v.astype(BF16)

    half = ATOMS // 2
    for p in range(2):
        for s in range(4):
            arrived(p, (ring[p] + 2) % 4, s, 2)
    for p in range(2):
        offer(p, 2)
        for i in range(2):
            c = remote(
                snd.at[p, 2, pl.ds(half * i, half)], mid.at[p, i], fs.at[p, 2 + i], fr.at[p, 2 + i], last_to[p](1 - 2 * i)
            )
            c.start()
            sent.append(c)
    for i, j in enumerate((1, 3)):
        for p in range(2):
            offer(p, j)
            c = remote(snd.at[p, j], rec.at[p, last[p]], fs.at[p, i], fr.at[p, i], last_to[p](1 - 2 * i))
            c.start()
            sent.append(c)
    for p in range(2):
        for i in range(2):
            remote(mid.at[p, i], mid.at[p, i], fs.at[p, 2 + i], fr.at[p, 2 + i], last_to[p](1)).wait_recv()
            c = remote(
                mid.at[p, i],
                rec.at[p, (last[p] + (3, 1)[i]) % 4, pl.ds(half * i, half)],
                fs.at[p, 4 + i],
                fr.at[p, 4 + i],
                last_to[p](1 - 2 * i),
            )
            c.start()
            sent.append(c)
    for p in range(2):
        for a, v in enumerate(contribution(p, 0)):
            sig[p, a] += v
    for p in range(2):
        for i in range(2):
            spot = rec.at[p, (last[p] + (3, 1)[i]) % 4]
            remote(spot, spot, fs.at[p, i], fr.at[p, i], last_to[p](1)).wait_recv()
            spot = rec.at[p, (last[p] + 2) % 4, pl.ds(half * i, half)]
            remote(spot, spot, fs.at[p, 4 + i], fr.at[p, 4 + i], last_to[p](1)).wait_recv()
        for a in range(ATOMS):
            total = sig[p, a]
            for j in range(1, 4):
                total = total + rec[p, (last[p] + j) % 4, a].astype(F32)
            wide[pl.ds(a * 2 * BLK + p, BLK, stride=2), :] = total
    out[...] = wide[...].astype(BF16)

    for c in sent:
        c.wait_send()
    for p in range(2):
        for k in range(3):

            @pl.when((z < 3) & (z - k >= 0))
            def _():
                climb(p, k, z - k).wait_send()

            @pl.when((z > 0) & (z + k <= 3))
            def _():
                descend(p, k, z + k).wait_send()

        for s in range(4):
            around(p, 0, s).wait_send()
            around(p, 1, s).wait_send()
            onward(p, s // 2, s).wait_send()


def self_energy(codes, key, where, mats, local):
    vmem = pl.BlockSpec(memory_space=pltpu.VMEM)
    dma = pltpu.SemaphoreType.DMA
    block = (BLK, SPAN)
    rows = DIRS * 7 * 16
    return pl.pallas_call(
        self_energy_kernel,
        out_shape=jax.ShapeDtypeStruct((2 * ATOMS * BLK, SPAN), BF16),
        in_specs=[vmem] * 5,
        out_specs=vmem,
        scratch_shapes=[
            pltpu.VMEM((65,) + block, BF16),
            pltpu.VMEM((65,) + block, BF16),
            pltpu.VMEM((2, 4, ATOMS) + block, BF16),
            pltpu.VMEM((2, 4, ATOMS) + block, BF16),
            pltpu.VMEM((2, 2, ATOMS // 2) + block, BF16),
            pltpu.VMEM((2, 4, 8, SPAN), jnp.int32),
            pltpu.SMEM((2, 4, 8, SPAN), jnp.int32),
            pltpu.VMEM((DIRS * 16, BLK), BF16),
            pltpu.VMEM((2, 4, DIRS * 16, BLK), BF16),
            pltpu.VMEM((2 * ORB, BLK, 2 * SPAN), BF16),
            pltpu.VMEM((ORB, rows, 2 * SPAN), F32),
            pltpu.VMEM((ORB, rows, 2 * SPAN), F32),
            pltpu.VMEM((2, BLK * 7 * 16, SPAN), F32),
            pltpu.VMEM((2, BLK * 16, SPAN), F32),
            pltpu.VMEM((7 * REMOTE, BLK, BLK), BF16),
            pltpu.VMEM((REMOTE,) + block, F32),
            pltpu.VMEM((2, ATOMS) + block, F32),
            pltpu.VMEM((2 * ATOMS * BLK, SPAN), F32),
            dma((10,)),
            dma((2, 2, 3)),
            dma((2, 2, 3)),
            dma((2, 3, 4)),
            dma((2, 3, 4)),
            dma((2, 6)),
            dma((2, 6)),
            dma((2, 3)),
            dma((2, 3)),
            dma((2, 3)),
            dma((2, 3)),
        ],
        compiler_params=pltpu.CompilerParams(
            collective_id=0, has_side_effects=True, vmem_limit_bytes=60 * 1024 * 1024
        ),
        name="self_energy",
    )(codes, key, where, mats, local)


def from_behind(value, axis, by):
    peers = lax.axis_size(axis)
    pairs = [(i, i + by) for i in range(peers) if 0 <= i + by < peers]
    return lax.ppermute(value, axis, pairs)


def plan(neighbours):
    me = lax.axis_index("atom")
    ids = neighbours.reshape(-1)
    owner, row = ids // ATOMS, ids % ATOMS
    remote = owner != me
    entry = jnp.arange(ENTRIES, dtype=jnp.int32)
    upto = (entry[:, None] <= entry[None, :]) & remote[:, None]
    rank = jnp.sum(upto.astype(jnp.int32), axis=0) - 1
    where = jnp.where(remote, -1, (entry // NBR) * ATOMS + row).reshape(1, ENTRIES)
    key = jnp.where(remote[:, None], rank[:, None] + 16 * jnp.arange(DIRS, dtype=jnp.int32)[None, :], -1)
    count = jnp.arange(REMOTE, dtype=jnp.int32)
    pick = (rank[None, :] == count[:, None]) & remote[None, :]
    packed = jnp.sum(jnp.where(pick, (ids * ATOMS + entry // NBR)[None, :], 0), axis=1)
    source, atom = packed // ATOMS, packed % ATOMS
    at_row, at_y, at_x, at_z = source % 4, (source // 4) % 4, (source // 16) % 4, source // 64
    before = jnp.concatenate([jnp.full((1,), -1, jnp.int32), atom[:-1]])
    slots = jnp.arange(ATOMS, dtype=jnp.int32)
    end = jnp.maximum(jnp.sum((atom[None, :] <= slots[:, None]).astype(jnp.int32), axis=1) - 1, 0)
    some = jnp.max((atom[None, :] == slots[:, None]).astype(jnp.int32), axis=1)
    lists = [
        (at_x * 4 + at_z) * 4 + at_row,
        (at_y * 4 + at_z) * 4 + at_row,
        at_y,
        at_x,
        (atom == before).astype(jnp.int32),
        end,
        some,
        some,
    ]
    codes = jnp.stack([jnp.pad(v, (0, SPAN - v.shape[0])) for v in lists])
    return codes, key.reshape(1, ENTRIES * DIRS), where


def rows_of(blocks):
    return blocks.transpose(0, 2, 3, 1, 4).reshape(2 * ATOMS * BLK, blocks.shape[-1])


def on_device(green, coupling, neighbours, shifts, weights):
    halo = from_behind(green[..., :MAXS], "energy", -1)
    local = convolve(rows_of(green), rows_of(halo), shifts, weights)
    codes, key, where = plan(neighbours)
    mats = coupling.reshape(ENTRIES * DIRS, BLK)
    out = self_energy(codes, key, where, mats, local.reshape(2, ATOMS, BLK, SPAN))
    return out.reshape(ATOMS, ORB, ORB, 2, SPAN).transpose(0, 3, 1, 2, 4)


def solution(mesh):
    placed = (P("atom", None, None, None, "energy"), P("atom", None), P("atom", None), P(), P())
    return jax.shard_map(
        on_device,
        mesh=mesh,
        in_specs=placed,
        out_specs=P("atom", None, None, None, "energy"),
        check_vma=False,
    )
```

```python
import functools

import jax
import jax.numpy as jnp
from jax import lax
from jax.experimental import pallas as pl
from jax.experimental.pallas import tpu as pltpu
from jax.sharding import PartitionSpec as P

ORB = 12
NBR = 24
DIRS = 3
NQ = 16
MAXS = 64
ATOMS = 4
REMOTE = 12
SPAN = 128
BLK = ORB * ORB
ENTRIES = ATOMS * NBR
F32 = jnp.float32
BF16 = jnp.bfloat16


def dot(a, b):
    return jnp.dot(a, b, preferred_element_type=F32)


def convolve(shifts, weights, mine, behind, wide, conv):
    lag = lax.broadcasted_iota(jnp.int32, (SPAN + MAXS, SPAN), 0) - lax.broadcasted_iota(
        jnp.int32, (SPAN + MAXS, SPAN), 1
    )
    band = jnp.zeros((SPAN + MAXS, SPAN), F32)
    for q in range(NQ):
        band = band + jnp.where(lag == shifts[q], weights[q], 0.0)
    high = band.astype(BF16)
    low = (band - high.astype(F32)).astype(BF16)
    wide[...] = (dot(mine, high[:SPAN]) + dot(mine, low[:SPAN])) + (
        dot(behind, high[SPAN:]) + dot(behind, low[SPAN:])
    )
    for p in range(2):
        for n in range(ATOMS):
            conv[p, n] = wide[pl.ds(2 * n * BLK + p, BLK, stride=2), :].astype(BF16)


def spreaders(qs):
    source = lax.broadcasted_iota(jnp.int32, (BLK, 2 * SPAN), 0)
    lane = lax.broadcasted_iota(jnp.int32, (BLK, 2 * SPAN), 1)
    group = (lane * 43691) >> 19
    inner = jnp.where(lane < BLK, lane - ORB * group, -BLK)
    group = jnp.where(lane < BLK, group, -BLK)
    for i in range(ORB):
        qs[i] = (source == ORB * i + group).astype(F32).astype(BF16)
        qs[ORB + i] = (source == ORB * i + inner).astype(F32).astype(BF16)


def expand(x, qs, r1, r2):
    rows = x.shape[0]
    for i in range(ORB):
        r1[i, pl.ds(0, rows), :] = dot(x, qs[i])
        r2[i, pl.ds(0, rows), :] = dot(x, qs[ORB + i])


def products(rows, r1, r2, kt):
    half = ORB // 2

    @pl.loop(0, rows // 8)
    def _(c):
        row = pl.multiple_of(c * 8, 8)
        for h in range(2):
            lanes = pl.ds(SPAN * h, SPAN)
            for g in range(2):
                left = [
                    [r1[half * g + i, pl.ds(rows * d + row, 8), lanes] for d in range(DIRS)] for i in range(half)
                ]
                for f in range(ORB):
                    right = [r2[f, pl.ds(rows * d + row, 8), lanes] for d in range(DIRS)]
                    for i in range(half):
                        total = left[i][0] * right[0] + left[i][1] * right[1] + left[i][2] * right[2]
                        kt[h, pl.ds(((half * g + i) * ORB + f) * rows + row, 8), :] = total


def pick_matrix(kt, first, stride):
    parts = [kt.at[h][pl.ds(first, BLK, stride=stride), :] for h in range(2)]
    return jnp.concatenate(parts, axis=1)[:, :BLK].astype(BF16)


def self_energy_kernel(
    shifts,
    weights,
    green,
    halo,
    codes,
    key,
    where,
    mats,
    out,
    local,
    buf0,
    buf1,
    rec,
    snd,
    mid,
    idv,
    ids,
    crem,
    crv,
    qs,
    r1,
    r2,
    kt,
    mt,
    kr,
    sst,
    sig,
    held,
    wide,
    ls,
    zs,
    zr,
    rs,
    rr,
    fs,
    fr,
    cs,
    cr,
    ps,
    pr,
):
    me = lax.axis_index("atom")
    z, x, y = me // 16, (me // 4) % 4, me % 4
    buf = (buf0, buf1)

    def device(dz, dx, dy):
        return {"atom": (z + dz) * 16 + ((x + dx) % 4) * 4 + (y + dy) % 4}

    def remote(src, dst, send, recv, to):
        return pltpu.make_async_remote_copy(
            src_ref=src,
            dst_ref=dst,
            send_sem=send,
            recv_sem=recv,
            device_id=to,
            device_id_type=pl.DeviceIdType.MESH,
        )

    ring = (x, y)
    ring_to = (lambda d: device(0, d, 0), lambda d: device(0, 0, d))
    last = (y, x)
    last_to = (ring_to[1], ring_to[0])
    down, up = device(-1, 0, 0), device(1, 0, 0)

    barrier = pltpu.get_barrier_semaphore()
    for to in (ring_to[0](1), ring_to[0](-1), ring_to[1](1), ring_to[1](-1)):
        pl.semaphore_signal(barrier, inc=1, device_id=to, device_id_type=pl.DeviceIdType.MESH)

    @pl.when(z > 0)
    def _():
        pl.semaphore_signal(barrier, inc=1, device_id=down, device_id_type=pl.DeviceIdType.MESH)

    @pl.when(z < 3)
    def _():
        pl.semaphore_signal(barrier, inc=1, device_id=up, device_id_type=pl.DeviceIdType.MESH)

    convolve(shifts, weights, green[...], halo[...], wide, local)
    row = lax.broadcasted_iota(jnp.int32, (DIRS * 16, ENTRIES * DIRS), 0)
    choice = (row == jnp.broadcast_to(key[...], row.shape)).astype(F32).astype(BF16)
    crem[...] = dot(choice, mats[...]).astype(BF16)
    pl.semaphore_wait(barrier, 6 - z // 3 - (3 - z) // 3)

    def place(p, r, s, h):
        return buf[p].at[pl.ds((r * 4 + s) * 4 + 2 * h, 2)]

    mine = [
        pltpu.make_async_copy(local.at[p], buf[p].at[pl.ds((ring[p] * 4 + z) * 4, 4)], ls.at[p]) for p in range(2)
    ]
    for c in mine:
        c.start()

    def ask(p, i, src, codes_src, slot, to):
        return [
            remote(codes_src, idv.at[p, slot], cs.at[p, i], cr.at[p, i], to),
            remote(src, crv.at[p, slot], ps.at[p, i], pr.at[p, i], to),
        ]

    for c in mine:
        c.wait()

    def climb(p, k, s, h):
        spot = place(p, ring[p], s, h)
        return remote(spot, spot, zs.at[p, 0, k, h], zr.at[p, 0, k, h], up)

    def descend(p, k, s, h):
        spot = place(p, ring[p], s, h)
        return remote(spot, spot, zs.at[p, 1, k, h], zr.at[p, 1, k, h], down)

    def around(p, i, s, h):
        spot = place(p, ring[p], s, h)
        return remote(spot, spot, rs.at[p, i, s, h], rr.at[p, i, s, h], ring_to[p](1 - 2 * i))

    def onward(p, s, h):
        spot = place(p, (ring[p] + (3, 1)[h]) % 4, s, h)
        return remote(spot, spot, rs.at[p, 2, s, h], rr.at[p, 2, s, h], ring_to[p](1 - 2 * h))

    def deliver(p, s, h):
        around(p, h, s, h).start()
        around(p, 1 - h, s, h).start()

    def arrived(p, r, s, i, h):
        spot = place(p, r, s, h)
        remote(spot, spot, rs.at[p, i, s, h], rr.at[p, i, s, h], ring_to[p](1)).wait_recv()

    def relay(p, s):
        for h in range(2):
            arrived(p, (ring[p] + (3, 1)[h]) % 4, s, h, h)
            onward(p, s, h).start()

    for h in range(2):
        for p in range(2):

            @pl.when(z < 3)
            def _():
                climb(p, 0, z, h).start()

            @pl.when(z > 0)
            def _():
                descend(p, 0, z, h).start()

            deliver(p, z, h)

    sent = []
    for p in range(2):
        for i, d in enumerate((1, -1)):
            for c in ask(p, i, crem, codes, last[p], last_to[p](d)):
                c.start()
                sent.append(c)
    own_codes = [pltpu.make_async_copy(codes, ids.at[p, last[p]], ls.at[2 + p]) for p in range(2)]
    for c in own_codes:
        c.start()

    def local_products():
        spreaders(qs)
        xs = mats[...]
        kd = ENTRIES * DIRS
        to = lax.broadcasted_iota(jnp.int32, (kd, kd), 0)
        at = lax.broadcasted_iota(jnp.int32, (kd, kd), 1)
        order = jnp.zeros((kd, kd), jnp.bool_)
        for d in range(DIRS):
            order = order | ((to >= ENTRIES * d) & (to < ENTRIES * (d + 1)) & (at == (to - ENTRIES * d) * DIRS + d))
        expand(dot(order.astype(F32).astype(BF16), xs).astype(BF16), qs, r1, r2)
        products(ENTRIES, r1, r2, kt)

    def local_sums():
        to = lax.broadcasted_iota(jnp.int32, (ATOMS * ATOMS, ENTRIES), 0)
        spread = (to == jnp.broadcast_to(where[...], to.shape)).astype(F32).astype(BF16)

        @pl.loop(0, BLK, step=4)
        def _(r):
            for u in range(4):
                at = pl.multiple_of((r + u) * ENTRIES, 8)
                both = jnp.concatenate([kt[h, pl.ds(at, ENTRIES), :] for h in range(2)], axis=1)
                summed = dot(spread, both.astype(BF16))
                for h in range(2):
                    mt[h, pl.ds((r + u) * 16, 16), :] = summed[:, SPAN * h : SPAN * (h + 1)]

    def local_energy():
        for a in range(ATOMS):
            acc = [jnp.zeros((BLK, SPAN), F32)] * 2
            for n in range(ATOMS):
                m = pick_matrix(mt, a * ATOMS + n, 16)
                for p in range(2):
                    acc[p] = acc[p] + dot(m, local[p, n])
            for p in range(2):
                sig[p, a] = acc[p]

    def forward_lists():
        for p in range(2):
            slot = (last[p] + 3) % 4
            for c in ask(p, 0, crem, codes, slot, last_to[p](-1)):
                c.wait_recv()
            for c in ask(p, 2, crv.at[p, slot], idv.at[p, slot], slot, last_to[p](1)):
                c.start()
                sent.append(c)

    def take_lists():
        moved = []
        for p in range(2):
            for i, j in ((1, 1), (2, 2)):
                slot = (last[p] + j) % 4
                for c in ask(p, i, crv.at[p, slot], idv.at[p, slot], slot, last_to[p](1)):
                    c.wait_recv()
            for j in range(1, 4):
                slot = (last[p] + j) % 4
                c = pltpu.make_async_copy(idv.at[p, slot], ids.at[p, slot], ls.at[4 + 3 * p + j - 1])
                c.start()
                moved.append(c)
        for c in own_codes + moved:
            c.wait()

    def remote_products():
        sets = [crem[...]] + [crv[p, (last[p] + j) % 4] for p in range(2) for j in range(1, 4)]
        xs = jnp.concatenate([v[16 * d : 16 * (d + 1)] for d in range(DIRS) for v in sets], axis=0)
        expand(xs, qs, r1, r2)
        products(7 * 16, r1, r2, kt)

    def remote_matrices():
        @pl.loop(0, 7 * REMOTE, step=2)
        def _(e):
            for u in range(2):
                kr[e + u] = pick_matrix(kt, (e + u) // REMOTE * 16 + (e + u) % REMOTE, 7 * 16)

    work = {
        0: [forward_lists, local_products],
        1: [local_sums, local_energy],
        2: [take_lists, remote_products],
        3: [remote_matrices],
    }
    for k in range(4):
        for piece in work[k]:
            piece()
        if k < 3:
            for p in range(2):
                for h in range(2):

                    @pl.when(z - 1 - k >= 0)
                    def _():
                        s = z - 1 - k
                        spot = place(p, ring[p], s, h)
                        remote(spot, spot, zs.at[p, 0, k, h], zr.at[p, 0, k, h], down).wait_recv()
                        if k < 2:

                            @pl.when(z < 3)
                            def _():
                                climb(p, k + 1, s, h).start()

                        deliver(p, s, h)

                    @pl.when(z + 1 + k <= 3)
                    def _():
                        s = z + 1 + k
                        spot = place(p, ring[p], s, h)
                        remote(spot, spot, zs.at[p, 1, k, h], zr.at[p, 1, k, h], up).wait_recv()
                        if k < 2:

                            @pl.when(z > 0)
                            def _():
                                descend(p, k + 1, s, h).start()

                        deliver(p, s, h)

        for p in range(2):
            if k == 0:
                relay(p, z)
            else:

                @pl.when(z - k >= 0)
                def _():
                    relay(p, z - k)

                @pl.when(z + k <= 3)
                def _():
                    relay(p, z + k)

    for p in range(2):
        buf[p][64] = jnp.zeros((BLK, SPAN), BF16)

    def contribution(p, j):
        slot = (last[p] + j) % 4
        q = 0 if j == 0 else 3 * p + j
        running = None
        for t in range(REMOTE):
            source = jnp.where(ids[p, slot, 2 + p, t] == last[p], ids[p, slot, p, t], 64)
            term = dot(kr[q * REMOTE + t], buf[p][source])
            keep = ids[p, slot, 4, t].astype(F32)
            running = term if running is None else keep * running + term
            sst[t] = running
        return [sst[ids[p, slot, 5, a]] * ids[p, slot, 6, a].astype(F32) for a in range(ATOMS)]

    def offer(p, j):
        for a, v in enumerate(contribution(p, j)):
            snd[p, j, a] = v.astype(BF16)

    half = ATOMS // 2
    top = (pl.ds(0, half), pl.ds(half, half))

    def send(p, i, n, src, dst):
        c = remote(src, dst, fs.at[p, i, n], fr.at[p, i, n], last_to[p](1 - 2 * i))
        c.start()
        sent.append(c)

    def taken(p, i, n, spot):
        remote(spot, spot, fs.at[p, i, n], fr.at[p, i, n], last_to[p](1)).wait_recv()

    for p in range(2):
        for s in range(4):
            for h in range(2):
                arrived(p, (ring[p] + (1, 3)[h]) % 4, s, 1 - h, h)
                arrived(p, (ring[p] + 2) % 4, s, 2, h)
        offer(p, 2)
        for i in range(2):
            send(p, i, 0, snd.at[p, 2, top[i]], mid.at[p, i])
        for i, j in enumerate((1, 3)):
            parts = contribution(p, j)
            for a in range(half * (1 - i), half * (2 - i)):
                snd[p, j, a] = parts[a].astype(BF16)
            send(p, i, 1, snd.at[p, j, top[1 - i]], rec.at[p, i, top[1 - i]])
            for a in range(half):
                held[p, i, a] = parts[half * i + a]
    for p in range(2):
        for a, v in enumerate(contribution(p, 0)):
            sig[p, a] += v
        for i, j in enumerate((1, 3)):
            taken(p, i, 0, mid.at[p, i])
            for a in range(half):
                snd[p, j, half * i + a] = (held[p, i, a] + mid[p, i, a].astype(F32)).astype(BF16)
            send(p, i, 2, snd.at[p, j, top[i]], rec.at[p, i, top[i]])
    for p in range(2):
        for i in range(2):
            taken(p, i, 1, rec.at[p, i, top[1 - i]])
            taken(p, i, 2, rec.at[p, i, top[i]])
        for a in range(ATOMS):
            total = sig[p, a] + (rec[p, 0, a].astype(F32) + rec[p, 1, a].astype(F32))
            out[pl.ds(a * 2 * BLK + p, BLK, stride=2), :] = total

    for c in sent:
        c.wait_send()
    for p in range(2):
        for k in range(3):

            @pl.when((z < 3) & (z - k >= 0))
            def _():
                for h in range(2):
                    climb(p, k, z - k, h).wait_send()

            @pl.when((z > 0) & (z + k <= 3))
            def _():
                for h in range(2):
                    descend(p, k, z + k, h).wait_send()

        for s in range(4):
            for h in range(2):
                around(p, 0, s, h).wait_send()
                around(p, 1, s, h).wait_send()
                onward(p, s, h).wait_send()


def self_energy(shifts, weights, green, halo, codes, key, where, mats):
    smem = pl.BlockSpec(memory_space=pltpu.SMEM)
    vmem = pl.BlockSpec(memory_space=pltpu.VMEM)
    dma = pltpu.SemaphoreType.DMA
    block = (BLK, SPAN)
    rows = DIRS * 7 * 16
    return pl.pallas_call(
        self_energy_kernel,
        out_shape=jax.ShapeDtypeStruct((2 * ATOMS * BLK, SPAN), F32),
        in_specs=[smem] * 2 + [vmem] * 6,
        out_specs=vmem,
        scratch_shapes=[
            pltpu.VMEM((2, ATOMS) + block, BF16),
            pltpu.VMEM((65,) + block, BF16),
            pltpu.VMEM((65,) + block, BF16),
            pltpu.VMEM((2, 2, ATOMS) + block, BF16),
            pltpu.VMEM((2, 4, ATOMS) + block, BF16),
            pltpu.VMEM((2, 2, ATOMS // 2) + block, BF16),
            pltpu.VMEM((2, 4, 8, SPAN), jnp.int32),
            pltpu.SMEM((2, 4, 8, SPAN), jnp.int32),
            pltpu.VMEM((DIRS * 16, BLK), BF16),
            pltpu.VMEM((2, 4, DIRS * 16, BLK), BF16),
            pltpu.VMEM((2 * ORB, BLK, 2 * SPAN), BF16),
            pltpu.VMEM((ORB, rows, 2 * SPAN), F32),
            pltpu.VMEM((ORB, rows, 2 * SPAN), F32),
            pltpu.VMEM((2, BLK * 7 * 16, SPAN), F32),
            pltpu.VMEM((2, BLK * 16, SPAN), F32),
            pltpu.VMEM((7 * REMOTE, BLK, BLK), BF16),
            pltpu.VMEM((REMOTE,) + block, F32),
            pltpu.VMEM((2, ATOMS) + block, F32),
            pltpu.VMEM((2, 2, ATOMS // 2) + block, F32),
            pltpu.VMEM((2 * ATOMS * BLK, SPAN), F32),
            dma((10,)),
            dma((2, 2, 3, 2)),
            dma((2, 2, 3, 2)),
            dma((2, 3, 4, 2)),
            dma((2, 3, 4, 2)),
            dma((2, 2, 3)),
            dma((2, 2, 3)),
            dma((2, 3)),
            dma((2, 3)),
            dma((2, 3)),
            dma((2, 3)),
        ],
        compiler_params=pltpu.CompilerParams(
            collective_id=0, has_side_effects=True, vmem_limit_bytes=60 * 1024 * 1024
        ),
        name="self_energy",
    )(shifts, weights, green, halo, codes, key, where, mats)


def from_behind(value, axis, by):
    peers = lax.axis_size(axis)
    pairs = [(i, i + by) for i in range(peers) if 0 <= i + by < peers]
    return lax.ppermute(value, axis, pairs)


def plan(neighbours):
    me = lax.axis_index("atom")
    ids = neighbours.reshape(-1)
    owner, row = ids // ATOMS, ids % ATOMS
    remote = owner != me
    entry = jnp.arange(ENTRIES, dtype=jnp.int32)
    upto = (entry[:, None] <= entry[None, :]) & remote[:, None]
    rank = jnp.sum(upto.astype(jnp.int32), axis=0) - 1
    where = jnp.where(remote, -1, (entry // NBR) * ATOMS + row).reshape(1, ENTRIES)
    key = jnp.where(remote[:, None], rank[:, None] + 16 * jnp.arange(DIRS, dtype=jnp.int32)[None, :], -1)
    count = jnp.arange(REMOTE, dtype=jnp.int32)
    pick = (rank[None, :] == count[:, None]) & remote[None, :]
    packed = jnp.sum(jnp.where(pick, (ids * ATOMS + entry // NBR)[None, :], 0), axis=1)
    source, atom = packed // ATOMS, packed % ATOMS
    at_row, at_y, at_x, at_z = source % 4, (source // 4) % 4, (source // 16) % 4, source // 64
    before = jnp.concatenate([jnp.full((1,), -1, jnp.int32), atom[:-1]])
    slots = jnp.arange(ATOMS, dtype=jnp.int32)
    end = jnp.maximum(jnp.sum((atom[None, :] <= slots[:, None]).astype(jnp.int32), axis=1) - 1, 0)
    some = jnp.max((atom[None, :] == slots[:, None]).astype(jnp.int32), axis=1)
    lists = [
        (at_x * 4 + at_z) * 4 + at_row,
        (at_y * 4 + at_z) * 4 + at_row,
        at_y,
        at_x,
        (atom == before).astype(jnp.int32),
        end,
        some,
        some,
    ]
    codes = jnp.stack([jnp.pad(v, (0, SPAN - v.shape[0])) for v in lists])
    return codes, key.reshape(1, ENTRIES * DIRS), where


def rows_of(blocks):
    return blocks.transpose(0, 2, 3, 1, 4).reshape(2 * ATOMS * BLK, blocks.shape[-1])


def on_device(green, coupling, neighbours, shifts, weights):
    halo = from_behind(green[..., :MAXS], "energy", -1)
    codes, key, where = plan(neighbours)
    mats = coupling.reshape(ENTRIES * DIRS, BLK)
    out = self_energy(shifts, weights, rows_of(green), rows_of(halo), codes, key, where, mats).astype(BF16)
    return out.reshape(ATOMS, ORB, ORB, 2, SPAN).transpose(0, 3, 1, 2, 4)


def solution(mesh):
    placed = (P("atom", None, None, None, "energy"), P("atom", None), P("atom", None), P(), P())
    return jax.shard_map(
        on_device,
        mesh=mesh,
        in_specs=placed,
        out_specs=P("atom", None, None, None, "energy"),
        check_vma=False,
    )
```

```python
import functools

import jax
import jax.numpy as jnp
from jax import lax
from jax.experimental import pallas as pl
from jax.experimental.pallas import tpu as pltpu
from jax.sharding import PartitionSpec as P

ORB = 12
NBR = 24
DIRS = 3
NQ = 16
MAXS = 64
ATOMS = 4
REMOTE = 12
SPAN = 128
BLK = ORB * ORB
ENTRIES = ATOMS * NBR
F32 = jnp.float32
BF16 = jnp.bfloat16


def dot(a, b):
    return jnp.dot(a, b, preferred_element_type=F32)


HALF = SPAN // 2


def lag_bands(shifts, weights):
    s = lax.broadcasted_iota(jnp.int32, (SPAN, SPAN), 0)
    t = lax.broadcasted_iota(jnp.int32, (SPAN, SPAN), 1)
    lag = jnp.where((s < HALF) == (t < HALF), s - t, -4 * SPAN)
    bands = []
    for extra in (0, HALF):
        band = jnp.zeros((SPAN, SPAN), F32)
        for q in range(NQ):
            band = band + jnp.where(lag == shifts[q] - extra, weights[q], 0.0)
        high = band.astype(BF16)
        bands.append((high, (band - high.astype(F32)).astype(BF16)))
    return bands


def convolve(near, far, bands):
    (near_high, near_low), (far_high, far_low) = bands
    total = (dot(near, near_high) + dot(near, near_low)) + (dot(far, far_high) + dot(far, far_low))
    return total.astype(BF16).reshape(ATOMS, BLK, SPAN)


def make_lists(neighbours, me):
    k = lax.broadcasted_iota(jnp.int32, (NBR, ENTRIES), 0)
    e = lax.broadcasted_iota(jnp.int32, (NBR, ENTRIES), 1)
    ids = neighbours.astype(F32).astype(BF16)
    flat = None
    for a in range(ATOMS):
        spread = dot(jnp.broadcast_to(ids[a : a + 1], (16, NBR)), (e == k + NBR * a).astype(F32).astype(BF16))
        flat = spread if flat is None else flat + spread
    ids = flat[:8].astype(jnp.int32)
    owner, row = ids >> 2, ids & 3
    entry = lax.broadcasted_iota(jnp.int32, (8, ENTRIES), 1)
    atom = (entry * 2731) >> 16
    remote = owner != me
    upto = lax.broadcasted_iota(jnp.int32, (ENTRIES, ENTRIES), 0) <= lax.broadcasted_iota(
        jnp.int32, (ENTRIES, ENTRIES), 1
    )
    ones = jnp.where(remote, 1.0, 0.0)
    both = jnp.concatenate([ones, ones], axis=0).astype(BF16)
    rank = dot(both, upto.astype(F32).astype(BF16))[:8].astype(jnp.int32) - 1
    key = jnp.where(remote, rank, -1)
    where = jnp.where(remote, -1, atom * ATOMS + row)
    x, y, z = (owner >> 2) & 3, owner & 3, owner >> 4
    kind = lax.broadcasted_iota(jnp.int32, (8, ENTRIES), 0)
    values = atom
    for i, v in enumerate(((x * 4 + z) * 4 + row, (y * 4 + z) * 4 + row, y, x)):
        values = jnp.where(kind == i, v, values)
    slot = lax.broadcasted_iota(jnp.int32, (SPAN, ENTRIES), 0)
    hit = (slot == jnp.broadcast_to(key[:1], slot.shape)).astype(F32).astype(BF16)
    values = values.astype(F32)
    values = jnp.concatenate([values, values], axis=0).astype(BF16)
    codes = lax.dot_general(values, hit, (((1,), (1,)), ((), ())), preferred_element_type=F32)
    return codes[:8].astype(jnp.int32), key[:1], where[:1]


def spreaders(qs):
    source = lax.broadcasted_iota(jnp.int32, (BLK, 2 * SPAN), 0)
    lane = lax.broadcasted_iota(jnp.int32, (BLK, 2 * SPAN), 1)
    group = (lane * 43691) >> 19
    inner = jnp.where(lane < BLK, lane - ORB * group, -BLK)
    group = jnp.where(lane < BLK, group, -BLK)
    for i in range(ORB):
        qs[i] = (source == ORB * i + group).astype(F32).astype(BF16)
        qs[ORB + i] = (source == ORB * i + inner).astype(F32).astype(BF16)


def expand(x, qs, r1, r2):
    rows = x.shape[0]
    for i in range(ORB):
        r1[i, pl.ds(0, rows), :] = dot(x, qs[i])
        r2[i, pl.ds(0, rows), :] = dot(x, qs[ORB + i])


def products(rows, r1, r2, kt, first, stop):
    half = ORB // 2

    @pl.loop(first, stop)
    def _(c):
        row = pl.multiple_of(c * 8, 8)
        for h in range(2):
            lanes = pl.ds(SPAN * h, SPAN)
            for g in range(2):
                left = [
                    [r1[half * g + i, pl.ds(rows * d + row, 8), lanes] for d in range(DIRS)] for i in range(half)
                ]
                for f in range(ORB):
                    right = [r2[f, pl.ds(rows * d + row, 8), lanes] for d in range(DIRS)]
                    for i in range(half):
                        total = left[i][0] * right[0] + left[i][1] * right[1] + left[i][2] * right[2]
                        kt[h, pl.ds(((half * g + i) * ORB + f) * rows + row, 8), :] = total


def pick_matrix(kt, first, stride):
    parts = [kt.at[h][pl.ds(first, BLK, stride=stride), :] for h in range(2)]
    return jnp.concatenate(parts, axis=1)[:, :BLK].astype(BF16)


def self_energy_kernel(
    shifts,
    weights,
    green,
    neighbours,
    mats,
    out,
    low,
    high,
    halo,
    local,
    buf0,
    buf1,
    rec,
    snd,
    mid,
    idv,
    ids,
    crem,
    crv,
    qs,
    r1,
    r2,
    kt,
    mt,
    kr,
    sst,
    sig,
    held,
    wide,
    sorted_mats,
    codes,
    hs,
    ls,
    zs,
    zr,
    rs,
    rr,
    fs,
    fr,
    cs,
    cr,
    ps,
    pr,
):
    me = lax.axis_index("atom")
    energy = lax.axis_index("energy")
    z, x, y = me // 16, (me // 4) % 4, me % 4
    buf = (buf0, buf1)

    def device(dz, dx, dy):
        return {"atom": (z + dz) * 16 + ((x + dx) % 4) * 4 + (y + dy) % 4}

    def remote(src, dst, send, recv, to):
        return pltpu.make_async_remote_copy(
            src_ref=src,
            dst_ref=dst,
            send_sem=send,
            recv_sem=recv,
            device_id=to,
            device_id_type=pl.DeviceIdType.MESH,
        )

    ring = (x, y)
    ring_to = (lambda d: device(0, d, 0), lambda d: device(0, 0, d))
    last = (y, x)
    last_to = (ring_to[1], ring_to[0])
    down, up = device(-1, 0, 0), device(1, 0, 0)

    barrier = pltpu.get_barrier_semaphore()
    for to in (ring_to[0](1), ring_to[0](-1), ring_to[1](1), ring_to[1](-1)):
        pl.semaphore_signal(barrier, inc=1, device_id=to, device_id_type=pl.DeviceIdType.MESH)

    @pl.when(z > 0)
    def _():
        pl.semaphore_signal(barrier, inc=1, device_id=down, device_id_type=pl.DeviceIdType.MESH)

    @pl.when(z < 3)
    def _():
        pl.semaphore_signal(barrier, inc=1, device_id=up, device_id_type=pl.DeviceIdType.MESH)

    @pl.when(energy > 0)
    def _():
        pl.semaphore_signal(
            barrier, inc=1, device_id={"energy": energy - 1}, device_id_type=pl.DeviceIdType.MESH
        )

    @pl.when(energy < 3)
    def _():
        pl.semaphore_signal(
            barrier, inc=1, device_id={"energy": energy + 1}, device_id_type=pl.DeviceIdType.MESH
        )

    wide[...] = green[...].astype(F32)
    real = wide[pl.ds(0, ATOMS * BLK, stride=2), :]
    imag = wide[pl.ds(1, ATOMS * BLK, stride=2), :]
    left = lax.broadcasted_iota(jnp.int32, real.shape, 1) < HALF
    low[...] = jnp.where(left, real, pltpu.roll(imag, HALF, 1)).astype(BF16)
    high[...] = jnp.where(left, pltpu.roll(real, HALF, 1), imag).astype(BF16)
    local[0] = convolve(low[...], high[...], lag_bands(shifts, weights))

    lists, key, where = make_lists(neighbours[...], me)
    codes[...] = lists

    kd = ENTRIES * DIRS
    to = lax.broadcasted_iota(jnp.int32, (kd, kd), 0)
    at = lax.broadcasted_iota(jnp.int32, (kd, kd), 1)
    order = jnp.zeros((kd, kd), jnp.bool_)
    for d in range(DIRS):
        order = order | ((to >= ENTRIES * d) & (to < ENTRIES * (d + 1)) & (at == (to - ENTRIES * d) * DIRS + d))
    sorted_mats[...] = dot(order.astype(F32).astype(BF16), mats[...]).astype(BF16)
    row = lax.broadcasted_iota(jnp.int32, (16, ENTRIES), 0)
    choice = (row == jnp.broadcast_to(key, row.shape)).astype(F32).astype(BF16)
    for d in range(DIRS):
        crem[pl.ds(16 * d, 16), :] = dot(choice, sorted_mats[pl.ds(ENTRIES * d, ENTRIES), :]).astype(BF16)
    pl.semaphore_wait(barrier, 8 - z // 3 - (3 - z) // 3 - energy // 3 - (3 - energy) // 3)

    def lower():
        return remote(low, halo, hs.at[0], hs.at[1], {"energy": energy - 1})

    @pl.when(energy > 0)
    def _():
        lower().start()

    @pl.when(energy == 3)
    def _():
        halo[...] = jnp.zeros_like(halo)

    def place(p, r, s, h):
        return buf[p].at[pl.ds((r * 4 + s) * 4 + 2 * h, 2)]

    def ask(p, i, src, codes_src, slot, to):
        return [
            remote(codes_src, idv.at[p, slot], cs.at[p, i], cr.at[p, i], to),
            remote(src, crv.at[p, slot], ps.at[p, i], pr.at[p, i], to),
        ]

    def climb(p, k, s, h):
        spot = place(p, ring[p], s, h)
        return remote(spot, spot, zs.at[p, 0, k, h], zr.at[p, 0, k, h], up)

    def descend(p, k, s, h):
        spot = place(p, ring[p], s, h)
        return remote(spot, spot, zs.at[p, 1, k, h], zr.at[p, 1, k, h], down)

    def around(p, i, s, h):
        spot = place(p, ring[p], s, h)
        return remote(spot, spot, rs.at[p, i, s, h], rr.at[p, i, s, h], ring_to[p](1 - 2 * i))

    def onward(p, s, h):
        spot = place(p, (ring[p] + (3, 1)[h]) % 4, s, h)
        return remote(spot, spot, rs.at[p, 2, s, h], rr.at[p, 2, s, h], ring_to[p](1 - 2 * h))

    def deliver(p, s, h):
        around(p, h, s, h).start()
        around(p, 1 - h, s, h).start()

    def arrived(p, r, s, i, h):
        spot = place(p, r, s, h)
        remote(spot, spot, rs.at[p, i, s, h], rr.at[p, i, s, h], ring_to[p](1)).wait_recv()

    def relay(p, s):
        for h in range(2):
            arrived(p, (ring[p] + (3, 1)[h]) % 4, s, h, h)
            onward(p, s, h).start()

    def begin(p):
        c = pltpu.make_async_copy(local.at[p], buf[p].at[pl.ds((ring[p] * 4 + z) * 4, 4)], ls.at[p])
        c.start()
        c.wait()
        for h in range(2):

            @pl.when(z < 3)
            def _():
                climb(p, 0, z, h).start()

            @pl.when(z > 0)
            def _():
                descend(p, 0, z, h).start()

            deliver(p, z, h)

    def lower_arrived():
        remote(low, halo, hs.at[0], hs.at[1], {"energy": energy + 1}).wait_recv()

    def begin_upper():
        local[1] = convolve(high[...], halo[...], lag_bands(shifts, weights))
        begin(1)

    begin(0)
    sent = []
    for p in range(2):
        for i, d in enumerate((1, -1)):
            for c in ask(p, i, crem, codes, last[p], last_to[p](d)):
                c.start()
                sent.append(c)
    own_codes = [pltpu.make_async_copy(codes, ids.at[p, last[p]], ls.at[2 + p]) for p in range(2)]
    for c in own_codes:
        c.start()

    def local_expand():
        spreaders(qs)
        expand(sorted_mats[...], qs, r1, r2)

    def local_products(n):
        products(ENTRIES, r1, r2, kt, 3 * n, 3 * n + 3)

    def local_sums(n):
        to = lax.broadcasted_iota(jnp.int32, (ATOMS * ATOMS, ENTRIES), 0)
        spread = (to == jnp.broadcast_to(where, to.shape)).astype(F32).astype(BF16)

        @pl.loop(36 * n, 36 * n + 36, step=4)
        def _(r):
            for u in range(4):
                at = pl.multiple_of((r + u) * ENTRIES, 8)
                both = jnp.concatenate([kt[h, pl.ds(at, ENTRIES), :] for h in range(2)], axis=1)
                summed = dot(spread, both.astype(BF16))
                for h in range(2):
                    mt[h, pl.ds((r + u) * 16, 16), :] = summed[:, SPAN * h : SPAN * (h + 1)]

    def local_energy():
        for a in range(ATOMS):
            acc = [jnp.zeros((BLK, SPAN), F32)] * 2
            for n in range(ATOMS):
                m = pick_matrix(mt, a * ATOMS + n, 16)
                for p in range(2):
                    acc[p] = acc[p] + dot(m, local[p, n])
            for p in range(2):
                sig[p, a] = acc[p]

    def forward_lists():
        for p in range(2):
            slot = (last[p] + 3) % 4
            for c in ask(p, 0, crem, codes, slot, last_to[p](-1)):
                c.wait_recv()
            for c in ask(p, 2, crv.at[p, slot], idv.at[p, slot], slot, last_to[p](1)):
                c.start()
                sent.append(c)

    def take_lists():
        moved = []
        for p in range(2):
            for i, j in ((1, 1), (2, 2)):
                slot = (last[p] + j) % 4
                for c in ask(p, i, crv.at[p, slot], idv.at[p, slot], slot, last_to[p](1)):
                    c.wait_recv()
            for j in range(1, 4):
                slot = (last[p] + j) % 4
                c = pltpu.make_async_copy(idv.at[p, slot], ids.at[p, slot], ls.at[4 + 3 * p + j - 1])
                c.start()
                moved.append(c)
        for c in own_codes + moved:
            c.wait()

    def remote_expand():
        sets = [crem[...]] + [crv[p, (last[p] + j) % 4] for p in range(2) for j in range(1, 4)]
        xs = jnp.concatenate([v[16 * d : 16 * (d + 1)] for d in range(DIRS) for v in sets], axis=0)
        expand(xs, qs, r1, r2)

    def remote_products(n):
        products(7 * 16, r1, r2, kt, (0, 5, 10)[n], (5, 10, 14)[n])

    def remote_matrices(n):
        @pl.loop(14 * n, 14 * n + 14, step=2)
        def _(e):
            for u in range(2):
                kr[e + u] = pick_matrix(kt, (e + u) // REMOTE * 16 + (e + u) % REMOTE, 7 * 16)

    def rise(p, k):
        for h in range(2):

            @pl.when(z - 1 - k >= 0)
            def _():
                s = z - 1 - k
                spot = place(p, ring[p], s, h)
                remote(spot, spot, zs.at[p, 0, k, h], zr.at[p, 0, k, h], down).wait_recv()
                if k < 2:

                    @pl.when(z < 3)
                    def _():
                        climb(p, k + 1, s, h).start()

                deliver(p, s, h)

            @pl.when(z + 1 + k <= 3)
            def _():
                s = z + 1 + k
                spot = place(p, ring[p], s, h)
                remote(spot, spot, zs.at[p, 1, k, h], zr.at[p, 1, k, h], up).wait_recv()
                if k < 2:

                    @pl.when(z > 0)
                    def _():
                        descend(p, k + 1, s, h).start()

                deliver(p, s, h)

    def pass_on(p, k):
        if k == 0:
            relay(p, z)
        else:

            @pl.when(z - k >= 0)
            def _():
                relay(p, z - k)

            @pl.when(z + k <= 3)
            def _():
                relay(p, z + k)

    @pl.when((energy == 0) | (energy == 2))
    def _():
        lower_arrived()
        begin_upper()

    @pl.when(energy == 3)
    def _():
        begin_upper()

    local_expand()
    forward_lists()
    local_products(0)
    rise(0, 0)
    local_products(1)
    pass_on(0, 0)
    local_products(2)

    @pl.when(energy == 1)
    def _():
        lower_arrived()
        begin_upper()

    local_products(3)
    rise(1, 0)
    local_sums(0)
    rise(0, 1)
    local_sums(1)
    pass_on(1, 0)
    local_sums(2)
    pass_on(0, 1)
    local_sums(3)
    rise(1, 1)
    take_lists()
    remote_expand()
    rise(0, 2)
    remote_products(0)
    pass_on(1, 1)
    remote_products(1)
    pass_on(0, 2)
    rise(1, 2)
    remote_products(2)
    pass_on(0, 3)
    remote_matrices(0)
    pass_on(1, 2)
    for n in range(1, 4):
        remote_matrices(n)
    pass_on(1, 3)
    for n in range(4, 6):
        remote_matrices(n)
    local_energy()

    for p in range(2):
        buf[p][64] = jnp.zeros((BLK, SPAN), BF16)

    def contribution(p, j):
        slot = (last[p] + j) % 4
        q = 0 if j == 0 else 3 * p + j
        running = None
        for t in range(REMOTE):
            source = jnp.where(ids[p, slot, 2 + p, t] == last[p], ids[p, slot, p, t], 64)
            term = dot(kr[q * REMOTE + t], buf[p][source])
            same = ids[p, slot, 4, t] == ids[p, slot, 4, max(t - 1, 0)]
            running = term if running is None else jnp.where(same, 1.0, 0.0) * running + term
            sst[t] = running
        atoms = [ids[p, slot, 4, t] for t in range(REMOTE)]
        parts = []
        for a in range(ATOMS):
            upto = sum(jnp.where(v <= a, 1, 0) for v in atoms)
            last_one = jnp.maximum(upto - 1, 0)
            some = jnp.where((upto > 0) & (ids[p, slot, 4, last_one] == a), 1.0, 0.0)
            parts.append(sst[last_one] * some)
        return parts

    def offer(p, j):
        for a, v in enumerate(contribution(p, j)):
            snd[p, j, a] = v.astype(BF16)

    half = ATOMS // 2
    top = (pl.ds(0, half), pl.ds(half, half))

    def send(p, i, n, src, dst):
        c = remote(src, dst, fs.at[p, i, n], fr.at[p, i, n], last_to[p](1 - 2 * i))
        c.start()
        sent.append(c)

    def taken(p, i, n, spot):
        remote(spot, spot, fs.at[p, i, n], fr.at[p, i, n], last_to[p](1)).wait_recv()

    for p in range(2):
        for s in range(4):
            for h in range(2):
                arrived(p, (ring[p] + (1, 3)[h]) % 4, s, 1 - h, h)
                arrived(p, (ring[p] + 2) % 4, s, 2, h)
        offer(p, 2)
        for i in range(2):
            send(p, i, 0, snd.at[p, 2, top[i]], mid.at[p, i])
        for i, j in enumerate((1, 3)):
            parts = contribution(p, j)
            for a in range(half * (1 - i), half * (2 - i)):
                snd[p, j, a] = parts[a].astype(BF16)
            send(p, i, 1, snd.at[p, j, top[1 - i]], rec.at[p, i, top[1 - i]])
            for a in range(half):
                held[p, i, a] = parts[half * i + a]
    for p in range(2):
        for a, v in enumerate(contribution(p, 0)):
            sig[p, a] += v
        for i, j in enumerate((1, 3)):
            taken(p, i, 0, mid.at[p, i])
            for a in range(half):
                snd[p, j, half * i + a] = (held[p, i, a] + mid[p, i, a].astype(F32)).astype(BF16)
            send(p, i, 2, snd.at[p, j, top[i]], rec.at[p, i, top[i]])
    for p in range(2):
        for i in range(2):
            taken(p, i, 1, rec.at[p, i, top[1 - i]])
            taken(p, i, 2, rec.at[p, i, top[i]])
        for a in range(ATOMS):
            sig[p, a] += rec[p, 0, a].astype(F32) + rec[p, 1, a].astype(F32)
    left = lax.broadcasted_iota(jnp.int32, (BLK, SPAN), 1) < HALF
    for a in range(ATOMS):
        lower_half, upper_half = sig[0, a], sig[1, a]
        out[pl.ds(a * 2 * BLK, BLK, stride=2), :] = jnp.where(left, lower_half, pltpu.roll(upper_half, HALF, 1))
        out[pl.ds(a * 2 * BLK + 1, BLK, stride=2), :] = jnp.where(left, pltpu.roll(lower_half, HALF, 1), upper_half)

    @pl.when(energy > 0)
    def _():
        lower().wait_send()

    for c in sent:
        c.wait_send()
    for p in range(2):
        for k in range(3):

            @pl.when((z < 3) & (z - k >= 0))
            def _():
                for h in range(2):
                    climb(p, k, z - k, h).wait_send()

            @pl.when((z > 0) & (z + k <= 3))
            def _():
                for h in range(2):
                    descend(p, k, z + k, h).wait_send()

        for s in range(4):
            for h in range(2):
                around(p, 0, s, h).wait_send()
                around(p, 1, s, h).wait_send()
                onward(p, s, h).wait_send()


def self_energy(shifts, weights, green, neighbours, mats):
    smem = pl.BlockSpec(memory_space=pltpu.SMEM)
    vmem = pl.BlockSpec(memory_space=pltpu.VMEM)
    dma = pltpu.SemaphoreType.DMA
    block = (BLK, SPAN)
    rows = DIRS * 7 * 16
    return pl.pallas_call(
        self_energy_kernel,
        out_shape=jax.ShapeDtypeStruct((2 * ATOMS * BLK, SPAN), F32),
        in_specs=[smem] * 2 + [vmem] * 3,
        out_specs=vmem,
        scratch_shapes=[
            pltpu.VMEM((ATOMS * BLK, SPAN), BF16),
            pltpu.VMEM((ATOMS * BLK, SPAN), BF16),
            pltpu.VMEM((ATOMS * BLK, SPAN), BF16),
            pltpu.VMEM((2, ATOMS) + block, BF16),
            pltpu.VMEM((65,) + block, BF16),
            pltpu.VMEM((65,) + block, BF16),
            pltpu.VMEM((2, 2, ATOMS) + block, BF16),
            pltpu.VMEM((2, 4, ATOMS) + block, BF16),
            pltpu.VMEM((2, 2, ATOMS // 2) + block, BF16),
            pltpu.VMEM((2, 4, 8, SPAN), jnp.int32),
            pltpu.SMEM((2, 4, 8, SPAN), jnp.int32),
            pltpu.VMEM((DIRS * 16, BLK), BF16),
            pltpu.VMEM((2, 4, DIRS * 16, BLK), BF16),
            pltpu.VMEM((2 * ORB, BLK, 2 * SPAN), BF16),
            pltpu.VMEM((ORB, rows, 2 * SPAN), F32),
            pltpu.VMEM((ORB, rows, 2 * SPAN), F32),
            pltpu.VMEM((2, BLK * 7 * 16, SPAN), F32),
            pltpu.VMEM((2, BLK * 16, SPAN), F32),
            pltpu.VMEM((7 * REMOTE, BLK, BLK), BF16),
            pltpu.VMEM((REMOTE,) + block, F32),
            pltpu.VMEM((2, ATOMS) + block, F32),
            pltpu.VMEM((2, 2, ATOMS // 2) + block, F32),
            pltpu.VMEM((2 * ATOMS * BLK, SPAN), F32),
            pltpu.VMEM((ENTRIES * DIRS, BLK), BF16),
            pltpu.VMEM((8, SPAN), jnp.int32),
            dma((2,)),
            dma((10,)),
            dma((2, 2, 3, 2)),
            dma((2, 2, 3, 2)),
            dma((2, 3, 4, 2)),
            dma((2, 3, 4, 2)),
            dma((2, 2, 3)),
            dma((2, 2, 3)),
            dma((2, 3)),
            dma((2, 3)),
            dma((2, 3)),
            dma((2, 3)),
        ],
        compiler_params=pltpu.CompilerParams(
            collective_id=0, has_side_effects=True, vmem_limit_bytes=60 * 1024 * 1024
        ),
        name="self_energy",
    )(shifts, weights, green, neighbours, mats)


def rows_of(blocks):
    return blocks.transpose(0, 2, 3, 1, 4).reshape(2 * ATOMS * BLK, blocks.shape[-1])


def on_device(green, coupling, neighbours, shifts, weights):
    mats = coupling.reshape(ENTRIES * DIRS, BLK)
    out = self_energy(shifts, weights, rows_of(green), neighbours, mats).astype(BF16)
    return out.reshape(ATOMS, ORB, ORB, 2, SPAN).transpose(0, 3, 1, 2, 4)


def solution(mesh):
    placed = (P("atom", None, None, None, "energy"), P("atom", None), P("atom", None), P(), P())
    return jax.shard_map(
        on_device,
        mesh=mesh,
        in_specs=placed,
        out_specs=P("atom", None, None, None, "energy"),
        check_vma=False,
    )
```

```python
import functools

import jax
import jax.numpy as jnp
from jax import lax
from jax.experimental import pallas as pl
from jax.experimental.pallas import tpu as pltpu
from jax.sharding import PartitionSpec as P

ORB = 12
NBR = 24
DIRS = 3
NQ = 16
MAXS = 64
ATOMS = 4
REMOTE = 12
SPAN = 128
BLK = ORB * ORB
ENTRIES = ATOMS * NBR
F32 = jnp.float32
BF16 = jnp.bfloat16


def dot(a, b):
    return jnp.dot(a, b, preferred_element_type=F32)


HALF = SPAN // 2


def lag_bands(shifts, weights):
    s = lax.broadcasted_iota(jnp.int32, (SPAN, SPAN), 0)
    t = lax.broadcasted_iota(jnp.int32, (SPAN, SPAN), 1)
    lag = jnp.where((s < HALF) == (t < HALF), s - t, -4 * SPAN)
    bands = []
    for extra in (0, HALF):
        band = jnp.zeros((SPAN, SPAN), F32)
        for q in range(NQ):
            band = band + jnp.where(lag == shifts[q] - extra, weights[q], 0.0)
        high = band.astype(BF16)
        bands.append((high, (band - high.astype(F32)).astype(BF16)))
    return bands


def convolve(near, far, bands):
    (near_high, near_low), (far_high, far_low) = bands
    total = (dot(near, near_high) + dot(near, near_low)) + (dot(far, far_high) + dot(far, far_low))
    return total.astype(BF16).reshape(ATOMS, BLK, SPAN)


def make_lists(neighbours, me):
    k = lax.broadcasted_iota(jnp.int32, (NBR, ENTRIES), 0)
    e = lax.broadcasted_iota(jnp.int32, (NBR, ENTRIES), 1)
    ids = neighbours.astype(F32).astype(BF16)
    flat = None
    for a in range(ATOMS):
        spread = dot(jnp.broadcast_to(ids[a : a + 1], (16, NBR)), (e == k + NBR * a).astype(F32).astype(BF16))
        flat = spread if flat is None else flat + spread
    ids = flat[:8].astype(jnp.int32)
    owner, row = ids >> 2, ids & 3
    entry = lax.broadcasted_iota(jnp.int32, (8, ENTRIES), 1)
    atom = (entry * 2731) >> 16
    remote = owner != me
    upto = lax.broadcasted_iota(jnp.int32, (ENTRIES, ENTRIES), 0) <= lax.broadcasted_iota(
        jnp.int32, (ENTRIES, ENTRIES), 1
    )
    ones = jnp.where(remote, 1.0, 0.0)
    both = jnp.concatenate([ones, ones], axis=0).astype(BF16)
    rank = dot(both, upto.astype(F32).astype(BF16))[:8].astype(jnp.int32) - 1
    key = jnp.where(remote, rank, -1)
    where = jnp.where(remote, -1, atom * ATOMS + row)
    x, y, z = (owner >> 2) & 3, owner & 3, owner >> 4
    kind = lax.broadcasted_iota(jnp.int32, (8, ENTRIES), 0)
    values = atom
    for i, v in enumerate(((x * 4 + z) * 4 + row, (y * 4 + z) * 4 + row, y, x)):
        values = jnp.where(kind == i, v, values)
    slot = lax.broadcasted_iota(jnp.int32, (SPAN, ENTRIES), 0)
    hit = (slot == jnp.broadcast_to(key[:1], slot.shape)).astype(F32).astype(BF16)
    values = values.astype(F32)
    values = jnp.concatenate([values, values], axis=0).astype(BF16)
    codes = lax.dot_general(values, hit, (((1,), (1,)), ((), ())), preferred_element_type=F32)
    return codes[:8].astype(jnp.int32), key[:1], where[:1]


def spreaders(qs):
    source = lax.broadcasted_iota(jnp.int32, (BLK, 2 * SPAN), 0)
    lane = lax.broadcasted_iota(jnp.int32, (BLK, 2 * SPAN), 1)
    group = (lane * 43691) >> 19
    inner = jnp.where(lane < BLK, lane - ORB * group, -BLK)
    group = jnp.where(lane < BLK, group, -BLK)
    for i in range(ORB):
        qs[i] = (source == ORB * i + group).astype(F32).astype(BF16)
        qs[ORB + i] = (source == ORB * i + inner).astype(F32).astype(BF16)


def expand(x, qs, r1, r2):
    rows = x.shape[0]
    for i in range(ORB):
        r1[i, pl.ds(0, rows), :] = dot(x, qs[i])
        r2[i, pl.ds(0, rows), :] = dot(x, qs[ORB + i])


def products(rows, r1, r2, kt, first, stop, step=None):
    step = step or rows
    half = ORB // 2

    @pl.loop(first, stop)
    def _(c):
        row = pl.multiple_of(c * 8, 8)
        for h in range(2):
            lanes = pl.ds(SPAN * h, SPAN)
            for g in range(2):
                left = [
                    [r1[half * g + i, pl.ds(rows * d + row, 8), lanes] for d in range(DIRS)] for i in range(half)
                ]
                for f in range(ORB):
                    right = [r2[f, pl.ds(rows * d + row, 8), lanes] for d in range(DIRS)]
                    for i in range(half):
                        total = left[i][0] * right[0] + left[i][1] * right[1] + left[i][2] * right[2]
                        kt[h, pl.ds(((half * g + i) * ORB + f) * step + row, 8), :] = total


def pick_matrix(kt, first, stride):
    parts = [kt.at[h][pl.ds(first, BLK, stride=stride), :] for h in range(2)]
    return jnp.concatenate(parts, axis=1)[:, :BLK].astype(BF16)


def self_energy_kernel(
    shifts,
    weights,
    green,
    neighbours,
    mats,
    out,
    low,
    high,
    halo,
    local,
    buf0,
    buf1,
    rec,
    snd,
    mid,
    idv,
    ids,
    crem,
    crv,
    qs,
    r1,
    r2,
    kt,
    mt,
    kr,
    sst,
    sig,
    held,
    wide,
    sorted_mats,
    codes,
    hs,
    ls,
    zs,
    zr,
    rs,
    rr,
    fs,
    fr,
    cs,
    cr,
    ps,
    pr,
):
    me = lax.axis_index("atom")
    energy = lax.axis_index("energy")
    z, x, y = me // 16, (me // 4) % 4, me % 4
    buf = (buf0, buf1)

    def device(dz, dx, dy):
        return {"atom": (z + dz) * 16 + ((x + dx) % 4) * 4 + (y + dy) % 4}

    def remote(src, dst, send, recv, to):
        return pltpu.make_async_remote_copy(
            src_ref=src,
            dst_ref=dst,
            send_sem=send,
            recv_sem=recv,
            device_id=to,
            device_id_type=pl.DeviceIdType.MESH,
        )

    ring = (x, y)
    ring_to = (lambda d: device(0, d, 0), lambda d: device(0, 0, d))
    last = (y, x)
    last_to = (ring_to[1], ring_to[0])
    down, up = device(-1, 0, 0), device(1, 0, 0)

    barrier = pltpu.get_barrier_semaphore()
    for to in (ring_to[0](1), ring_to[0](-1), ring_to[1](1), ring_to[1](-1)):
        pl.semaphore_signal(barrier, inc=1, device_id=to, device_id_type=pl.DeviceIdType.MESH)

    @pl.when(z > 0)
    def _():
        pl.semaphore_signal(barrier, inc=1, device_id=down, device_id_type=pl.DeviceIdType.MESH)

    @pl.when(z < 3)
    def _():
        pl.semaphore_signal(barrier, inc=1, device_id=up, device_id_type=pl.DeviceIdType.MESH)

    @pl.when(energy > 0)
    def _():
        pl.semaphore_signal(
            barrier, inc=1, device_id={"energy": energy - 1}, device_id_type=pl.DeviceIdType.MESH
        )

    @pl.when(energy < 3)
    def _():
        pl.semaphore_signal(
            barrier, inc=1, device_id={"energy": energy + 1}, device_id_type=pl.DeviceIdType.MESH
        )

    wide[...] = green[...].astype(F32)
    real = wide[pl.ds(0, ATOMS * BLK, stride=2), :]
    imag = wide[pl.ds(1, ATOMS * BLK, stride=2), :]
    left = lax.broadcasted_iota(jnp.int32, real.shape, 1) < HALF
    low[...] = jnp.where(left, real, pltpu.roll(imag, HALF, 1)).astype(BF16)
    high[...] = jnp.where(left, pltpu.roll(real, HALF, 1), imag).astype(BF16)
    lower_block = convolve(low[...], high[...], lag_bands(shifts, weights))
    local[0] = lower_block
    buf0[pl.ds((x * 4 + z) * 4, 4)] = lower_block

    lists, key, where = make_lists(neighbours[...], me)
    codes[...] = lists

    kd = ENTRIES * DIRS
    to = lax.broadcasted_iota(jnp.int32, (kd, kd), 0)
    at = lax.broadcasted_iota(jnp.int32, (kd, kd), 1)
    order = jnp.zeros((kd, kd), jnp.bool_)
    for d in range(DIRS):
        order = order | ((to >= ENTRIES * d) & (to < ENTRIES * (d + 1)) & (at == (to - ENTRIES * d) * DIRS + d))
    sorted_mats[...] = dot(order.astype(F32).astype(BF16), mats[...]).astype(BF16)
    row = lax.broadcasted_iota(jnp.int32, (16, ENTRIES), 0)
    choice = (row == jnp.broadcast_to(key, row.shape)).astype(F32).astype(BF16)
    for d in range(DIRS):
        crem[pl.ds(16 * d, 16), :] = dot(choice, sorted_mats[pl.ds(ENTRIES * d, ENTRIES), :]).astype(BF16)
    spreaders(qs)
    expand(sorted_mats[...], qs, r1, r2)
    pl.semaphore_wait(barrier, 8 - z // 3 - (3 - z) // 3 - energy // 3 - (3 - energy) // 3)

    def lower():
        return remote(low, halo, hs.at[0], hs.at[1], {"energy": energy - 1})

    @pl.when(energy > 0)
    def _():
        lower().start()

    @pl.when(energy == 3)
    def _():
        halo[...] = jnp.zeros_like(halo)

    def place(p, r, s, h):
        return buf[p].at[pl.ds((r * 4 + s) * 4 + 2 * h, 2)]

    def ask(p, i, src, codes_src, slot, to):
        return [
            remote(codes_src, idv.at[p, slot], cs.at[p, i], cr.at[p, i], to),
            remote(src, crv.at[p, slot], ps.at[p, i], pr.at[p, i], to),
        ]

    def climb(p, k, s, h):
        spot = place(p, ring[p], s, h)
        return remote(spot, spot, zs.at[p, 0, k, h], zr.at[p, 0, k, h], up)

    def descend(p, k, s, h):
        spot = place(p, ring[p], s, h)
        return remote(spot, spot, zs.at[p, 1, k, h], zr.at[p, 1, k, h], down)

    def around(p, i, s, h):
        spot = place(p, ring[p], s, h)
        return remote(spot, spot, rs.at[p, i, s, h], rr.at[p, i, s, h], ring_to[p](1 - 2 * i))

    def onward(p, s, h):
        spot = place(p, (ring[p] + (3, 1)[h]) % 4, s, h)
        return remote(spot, spot, rs.at[p, 2, s, h], rr.at[p, 2, s, h], ring_to[p](1 - 2 * h))

    def deliver(p, s, h):
        around(p, h, s, h).start()
        around(p, 1 - h, s, h).start()

    def arrived(p, r, s, i, h):
        spot = place(p, r, s, h)
        remote(spot, spot, rs.at[p, i, s, h], rr.at[p, i, s, h], ring_to[p](1)).wait_recv()

    def relay(p, s):
        for h in range(2):
            arrived(p, (ring[p] + (3, 1)[h]) % 4, s, h, h)
            onward(p, s, h).start()

    def begin(p):
        if p == 1:
            c = pltpu.make_async_copy(local.at[p], buf[p].at[pl.ds((ring[p] * 4 + z) * 4, 4)], ls.at[p])
            c.start()
            c.wait()
        for h in range(2):

            @pl.when(z < 3)
            def _():
                climb(p, 0, z, h).start()

            @pl.when(z > 0)
            def _():
                descend(p, 0, z, h).start()

            deliver(p, z, h)

    def lower_arrived():
        remote(low, halo, hs.at[0], hs.at[1], {"energy": energy + 1}).wait_recv()

    def begin_upper():
        local[1] = convolve(high[...], halo[...], lag_bands(shifts, weights))
        begin(1)

    begin(0)
    sent = []
    for p in range(2):
        for i, d in enumerate((1, -1)):
            for c in ask(p, i, crem, codes, last[p], last_to[p](d)):
                c.start()
                sent.append(c)
    own_codes = [pltpu.make_async_copy(codes, ids.at[p, last[p]], ls.at[2 + p]) for p in range(2)]
    for c in own_codes:
        c.start()

    def local_products(n):
        products(ENTRIES, r1, r2, kt, 3 * n, 3 * n + 3)

    def local_sums(n):
        to = lax.broadcasted_iota(jnp.int32, (ATOMS * ATOMS, ENTRIES), 0)
        spread = (to == jnp.broadcast_to(where, to.shape)).astype(F32).astype(BF16)

        @pl.loop(36 * n, 36 * n + 36, step=12)
        def _(r):
            for u in range(12):
                at = pl.multiple_of((r + u) * ENTRIES, 8)
                both = jnp.concatenate([kt[h, pl.ds(at, ENTRIES), :] for h in range(2)], axis=1)
                summed = dot(spread, both.astype(BF16))
                for h in range(2):
                    mt[h, pl.ds((r + u) * 17, 16), :] = summed[:, SPAN * h : SPAN * (h + 1)]

    def local_energy():
        for a in range(ATOMS):
            acc = [jnp.zeros((BLK, SPAN), F32)] * 2
            for n in range(ATOMS):
                m = pick_matrix(mt, a * ATOMS + n, 17)
                for p in range(2):
                    acc[p] = acc[p] + dot(m, local[p, n])
            for p in range(2):
                sig[p, a] = acc[p]

    def forward_lists():
        for p in range(2):
            slot = (last[p] + 3) % 4
            for c in ask(p, 0, crem, codes, slot, last_to[p](-1)):
                c.wait_recv()
            for c in ask(p, 2, crv.at[p, slot], idv.at[p, slot], slot, last_to[p](1)):
                c.start()
                sent.append(c)

    def take_lists():
        moved = []
        for p in range(2):
            for i, j in ((1, 1), (2, 2)):
                slot = (last[p] + j) % 4
                for c in ask(p, i, crv.at[p, slot], idv.at[p, slot], slot, last_to[p](1)):
                    c.wait_recv()
            for j in range(1, 4):
                slot = (last[p] + j) % 4
                c = pltpu.make_async_copy(idv.at[p, slot], ids.at[p, slot], ls.at[4 + 3 * p + j - 1])
                c.start()
                moved.append(c)
        for c in own_codes + moved:
            c.wait()

    def remote_expand():
        sets = [crem[...]] + [crv[p, (last[p] + j) % 4] for p in range(2) for j in range(1, 4)]
        xs = jnp.concatenate([v[16 * d : 16 * (d + 1)] for d in range(DIRS) for v in sets], axis=0)
        expand(xs, qs, r1, r2)

    def remote_products(n):
        products(7 * 16, r1, r2, kt, (0, 5, 10)[n], (5, 10, 14)[n], 7 * 16 + 1)

    def remote_matrices(n):
        @pl.loop(14 * n, 14 * n + 14, step=7)
        def _(e):
            for u in range(7):
                kr[e + u] = pick_matrix(kt, (e + u) // REMOTE * 16 + (e + u) % REMOTE, 7 * 16 + 1)

    def rise(p, k):
        for h in range(2):

            @pl.when(z - 1 - k >= 0)
            def _():
                s = z - 1 - k
                spot = place(p, ring[p], s, h)
                remote(spot, spot, zs.at[p, 0, k, h], zr.at[p, 0, k, h], down).wait_recv()
                if k < 2:

                    @pl.when(z < 3)
                    def _():
                        climb(p, k + 1, s, h).start()

                deliver(p, s, h)

            @pl.when(z + 1 + k <= 3)
            def _():
                s = z + 1 + k
                spot = place(p, ring[p], s, h)
                remote(spot, spot, zs.at[p, 1, k, h], zr.at[p, 1, k, h], up).wait_recv()
                if k < 2:

                    @pl.when(z > 0)
                    def _():
                        descend(p, k + 1, s, h).start()

                deliver(p, s, h)

    def pass_on(p, k):
        if k == 0:
            relay(p, z)
        else:

            @pl.when(z - k >= 0)
            def _():
                relay(p, z - k)

            @pl.when(z + k <= 3)
            def _():
                relay(p, z + k)

    @pl.when((energy == 0) | (energy == 2))
    def _():
        lower_arrived()
        begin_upper()

    @pl.when(energy == 3)
    def _():
        begin_upper()

    forward_lists()
    local_products(0)
    rise(0, 0)
    local_products(1)
    pass_on(0, 0)
    local_products(2)

    @pl.when(energy == 1)
    def _():
        lower_arrived()
        begin_upper()

    local_products(3)
    rise(1, 0)
    local_sums(0)
    rise(0, 1)
    local_sums(1)
    pass_on(1, 0)
    local_sums(2)
    pass_on(0, 1)
    local_sums(3)
    rise(1, 1)
    take_lists()
    remote_expand()
    rise(0, 2)
    remote_products(0)
    pass_on(1, 1)
    remote_products(1)
    pass_on(0, 2)
    rise(1, 2)
    remote_products(2)
    pass_on(0, 3)
    remote_matrices(0)
    pass_on(1, 2)
    for n in range(1, 4):
        remote_matrices(n)
    pass_on(1, 3)
    for n in range(4, 6):
        remote_matrices(n)
    local_energy()

    for p in range(2):
        buf[p][64] = jnp.zeros((BLK, SPAN), BF16)

    def contribution(p, j):
        slot = (last[p] + j) % 4
        q = 0 if j == 0 else 3 * p + j
        running = None
        for t in range(REMOTE):
            source = jnp.where(ids[p, slot, 2 + p, t] == last[p], ids[p, slot, p, t], 64)
            term = dot(kr[q * REMOTE + t], buf[p][source])
            same = ids[p, slot, 4, t] == ids[p, slot, 4, max(t - 1, 0)]
            running = term if running is None else jnp.where(same, 1.0, 0.0) * running + term
            sst[t] = running
        atoms = [ids[p, slot, 4, t] for t in range(REMOTE)]
        parts = []
        for a in range(ATOMS):
            upto = sum(jnp.where(v <= a, 1, 0) for v in atoms)
            last_one = jnp.maximum(upto - 1, 0)
            some = jnp.where((upto > 0) & (ids[p, slot, 4, last_one] == a), 1.0, 0.0)
            parts.append(sst[last_one] * some)
        return parts

    def offer(p, j):
        for a, v in enumerate(contribution(p, j)):
            snd[p, j, a] = v.astype(BF16)

    half = ATOMS // 2
    top = (pl.ds(0, half), pl.ds(half, half))

    def send(p, i, n, src, dst):
        c = remote(src, dst, fs.at[p, i, n], fr.at[p, i, n], last_to[p](1 - 2 * i))
        c.start()
        sent.append(c)

    def taken(p, i, n, spot):
        remote(spot, spot, fs.at[p, i, n], fr.at[p, i, n], last_to[p](1)).wait_recv()

    for p in range(2):
        for s in range(4):
            for h in range(2):
                arrived(p, (ring[p] + (1, 3)[h]) % 4, s, 1 - h, h)
                arrived(p, (ring[p] + 2) % 4, s, 2, h)
        offer(p, 2)
        for i in range(2):
            send(p, i, 0, snd.at[p, 2, top[i]], mid.at[p, i])
        for i, j in enumerate((1, 3)):
            parts = contribution(p, j)
            for a in range(half * (1 - i), half * (2 - i)):
                snd[p, j, a] = parts[a].astype(BF16)
            send(p, i, 1, snd.at[p, j, top[1 - i]], rec.at[p, i, top[1 - i]])
            for a in range(half):
                held[p, i, a] = parts[half * i + a]
    for p in range(2):
        for a, v in enumerate(contribution(p, 0)):
            sig[p, a] += v
        for i, j in enumerate((1, 3)):
            taken(p, i, 0, mid.at[p, i])
            for a in range(half):
                snd[p, j, half * i + a] = (held[p, i, a] + mid[p, i, a].astype(F32)).astype(BF16)
            send(p, i, 2, snd.at[p, j, top[i]], rec.at[p, i, top[i]])
    for p in range(2):
        for i in range(2):
            taken(p, i, 1, rec.at[p, i, top[1 - i]])
            taken(p, i, 2, rec.at[p, i, top[i]])
        for a in range(ATOMS):
            sig[p, a] += rec[p, 0, a].astype(F32) + rec[p, 1, a].astype(F32)
    left = lax.broadcasted_iota(jnp.int32, (BLK, SPAN), 1) < HALF
    for a in range(ATOMS):
        lower_half, upper_half = sig[0, a], sig[1, a]
        out[pl.ds(a * 2 * BLK, BLK, stride=2), :] = jnp.where(left, lower_half, pltpu.roll(upper_half, HALF, 1))
        out[pl.ds(a * 2 * BLK + 1, BLK, stride=2), :] = jnp.where(left, pltpu.roll(lower_half, HALF, 1), upper_half)

    @pl.when(energy > 0)
    def _():
        lower().wait_send()

    for c in sent:
        c.wait_send()
    for p in range(2):
        for k in range(3):

            @pl.when((z < 3) & (z - k >= 0))
            def _():
                for h in range(2):
                    climb(p, k, z - k, h).wait_send()

            @pl.when((z > 0) & (z + k <= 3))
            def _():
                for h in range(2):
                    descend(p, k, z + k, h).wait_send()

        for s in range(4):
            for h in range(2):
                around(p, 0, s, h).wait_send()
                around(p, 1, s, h).wait_send()
                onward(p, s, h).wait_send()


def self_energy(shifts, weights, green, neighbours, mats):
    smem = pl.BlockSpec(memory_space=pltpu.SMEM)
    vmem = pl.BlockSpec(memory_space=pltpu.VMEM)
    dma = pltpu.SemaphoreType.DMA
    block = (BLK, SPAN)
    rows = DIRS * 7 * 16
    return pl.pallas_call(
        self_energy_kernel,
        out_shape=jax.ShapeDtypeStruct((2 * ATOMS * BLK, SPAN), F32),
        in_specs=[smem] * 2 + [vmem] * 3,
        out_specs=vmem,
        scratch_shapes=[
            pltpu.VMEM((ATOMS * BLK, SPAN), BF16),
            pltpu.VMEM((ATOMS * BLK, SPAN), BF16),
            pltpu.VMEM((ATOMS * BLK, SPAN), BF16),
            pltpu.VMEM((2, ATOMS) + block, BF16),
            pltpu.VMEM((65,) + block, BF16),
            pltpu.VMEM((65,) + block, BF16),
            pltpu.VMEM((2, 2, ATOMS) + block, BF16),
            pltpu.VMEM((2, 4, ATOMS) + block, BF16),
            pltpu.VMEM((2, 2, ATOMS // 2) + block, BF16),
            pltpu.VMEM((2, 4, 8, SPAN), jnp.int32),
            pltpu.SMEM((2, 4, 8, SPAN), jnp.int32),
            pltpu.VMEM((DIRS * 16, BLK), BF16),
            pltpu.VMEM((2, 4, DIRS * 16, BLK), BF16),
            pltpu.VMEM((2 * ORB, BLK, 2 * SPAN), BF16),
            pltpu.VMEM((ORB, rows, 2 * SPAN), F32),
            pltpu.VMEM((ORB, rows, 2 * SPAN), F32),
            pltpu.VMEM((2, BLK * (7 * 16 + 1), SPAN), F32),
            pltpu.VMEM((2, BLK * 17, SPAN), F32),
            pltpu.VMEM((7 * REMOTE, BLK, BLK), BF16),
            pltpu.VMEM((REMOTE,) + block, F32),
            pltpu.VMEM((2, ATOMS) + block, F32),
            pltpu.VMEM((2, 2, ATOMS // 2) + block, F32),
            pltpu.VMEM((2 * ATOMS * BLK, SPAN), F32),
            pltpu.VMEM((ENTRIES * DIRS, BLK), BF16),
            pltpu.VMEM((8, SPAN), jnp.int32),
            dma((2,)),
            dma((10,)),
            dma((2, 2, 3, 2)),
            dma((2, 2, 3, 2)),
            dma((2, 3, 4, 2)),
            dma((2, 3, 4, 2)),
            dma((2, 2, 3)),
            dma((2, 2, 3)),
            dma((2, 3)),
            dma((2, 3)),
            dma((2, 3)),
            dma((2, 3)),
        ],
        compiler_params=pltpu.CompilerParams(
            collective_id=0, has_side_effects=True, vmem_limit_bytes=60 * 1024 * 1024
        ),
        name="self_energy",
    )(shifts, weights, green, neighbours, mats)


def rows_of(blocks):
    return blocks.transpose(0, 2, 3, 1, 4).reshape(2 * ATOMS * BLK, blocks.shape[-1])


def on_device(green, coupling, neighbours, shifts, weights):
    mats = coupling.reshape(ENTRIES * DIRS, BLK)
    out = self_energy(shifts, weights, rows_of(green), neighbours, mats).astype(BF16)
    return out.reshape(ATOMS, ORB, ORB, 2, SPAN).transpose(0, 3, 1, 2, 4)


def solution(mesh):
    placed = (P("atom", None, None, None, "energy"), P("atom", None), P("atom", None), P(), P())
    return jax.shard_map(
        on_device,
        mesh=mesh,
        in_specs=placed,
        out_specs=P("atom", None, None, None, "energy"),
        check_vma=False,
    )
```

```python
import functools

import jax
import jax.numpy as jnp
from jax import lax
from jax.experimental import pallas as pl
from jax.experimental.pallas import tpu as pltpu
from jax.sharding import PartitionSpec as P

ORB = 12
NBR = 24
DIRS = 3
NQ = 16
MAXS = 64
ATOMS = 4
REMOTE = 12
SPAN = 128
BLK = ORB * ORB
ENTRIES = ATOMS * NBR
F32 = jnp.float32
BF16 = jnp.bfloat16


def dot(a, b):
    return jnp.dot(a, b, preferred_element_type=F32)


HALF = SPAN // 2


def lag_bands(shifts, weights):
    s = lax.broadcasted_iota(jnp.int32, (SPAN, SPAN), 0)
    t = lax.broadcasted_iota(jnp.int32, (SPAN, SPAN), 1)
    lag = jnp.where((s < HALF) == (t < HALF), s - t, -4 * SPAN)
    bands = []
    for extra in (0, HALF):
        band = jnp.zeros((SPAN, SPAN), F32)
        for q in range(NQ):
            band = band + jnp.where(lag == shifts[q] - extra, weights[q], 0.0)
        high = band.astype(BF16)
        bands.append((high, (band - high.astype(F32)).astype(BF16)))
    return bands


def convolve(near, far, bands):
    (near_high, near_low), (far_high, far_low) = bands
    total = (dot(near, near_high) + dot(near, near_low)) + (dot(far, far_high) + dot(far, far_low))
    return total.astype(BF16).reshape(ATOMS, BLK, SPAN)


def make_lists(neighbours, me):
    k = lax.broadcasted_iota(jnp.int32, (NBR, ENTRIES), 0)
    e = lax.broadcasted_iota(jnp.int32, (NBR, ENTRIES), 1)
    ids = neighbours.astype(F32).astype(BF16)
    flat = None
    for a in range(ATOMS):
        spread = dot(jnp.broadcast_to(ids[a : a + 1], (16, NBR)), (e == k + NBR * a).astype(F32).astype(BF16))
        flat = spread if flat is None else flat + spread
    ids = flat[:8].astype(jnp.int32)
    owner, row = ids >> 2, ids & 3
    entry = lax.broadcasted_iota(jnp.int32, (8, ENTRIES), 1)
    atom = (entry * 2731) >> 16
    remote = owner != me
    upto = lax.broadcasted_iota(jnp.int32, (ENTRIES, ENTRIES), 0) <= lax.broadcasted_iota(
        jnp.int32, (ENTRIES, ENTRIES), 1
    )
    ones = jnp.where(remote, 1.0, 0.0)
    both = jnp.concatenate([ones, ones], axis=0).astype(BF16)
    rank = dot(both, upto.astype(F32).astype(BF16))[:8].astype(jnp.int32) - 1
    key = jnp.where(remote, rank, -1)
    where = jnp.where(remote, -1, atom * ATOMS + row)
    x, y, z = (owner >> 2) & 3, owner & 3, owner >> 4
    kind = lax.broadcasted_iota(jnp.int32, (8, ENTRIES), 0)
    values = atom
    for i, v in enumerate(((x * 4 + z) * 4 + row, (y * 4 + z) * 4 + row, y, x)):
        values = jnp.where(kind == i, v, values)
    slot = lax.broadcasted_iota(jnp.int32, (SPAN, ENTRIES), 0)
    hit = (slot == jnp.broadcast_to(key[:1], slot.shape)).astype(F32).astype(BF16)
    values = values.astype(F32)
    values = jnp.concatenate([values, values], axis=0).astype(BF16)
    codes = lax.dot_general(values, hit, (((1,), (1,)), ((), ())), preferred_element_type=F32)
    return codes[:8].astype(jnp.int32), key[:1], where[:1]


def spreaders(qs):
    source = lax.broadcasted_iota(jnp.int32, (BLK, 2 * SPAN), 0)
    lane = lax.broadcasted_iota(jnp.int32, (BLK, 2 * SPAN), 1)
    group = (lane * 43691) >> 19
    inner = jnp.where(lane < BLK, lane - ORB * group, -BLK)
    group = jnp.where(lane < BLK, group, -BLK)
    for i in range(ORB):
        qs[i] = (source == ORB * i + group).astype(F32).astype(BF16)
        qs[ORB + i] = (source == ORB * i + inner).astype(F32).astype(BF16)


def expand(x, qs, r1, r2):
    rows = x.shape[0]
    for i in range(ORB):
        r1[i, pl.ds(0, rows), :] = dot(x, qs[i])
        r2[i, pl.ds(0, rows), :] = dot(x, qs[ORB + i])


def products(rows, r1, r2, kt, first, stop, step=None):
    step = step or rows
    half = ORB // 2

    @pl.loop(first, stop)
    def _(c):
        row = pl.multiple_of(c * 8, 8)
        for h in range(2):
            lanes = pl.ds(SPAN * h, SPAN)
            for g in range(2):
                left = [
                    [r1[half * g + i, pl.ds(rows * d + row, 8), lanes] for d in range(DIRS)] for i in range(half)
                ]
                for f in range(ORB):
                    right = [r2[f, pl.ds(rows * d + row, 8), lanes] for d in range(DIRS)]
                    for i in range(half):
                        total = left[i][0] * right[0] + left[i][1] * right[1] + left[i][2] * right[2]
                        kt[h, pl.ds(((half * g + i) * ORB + f) * step + row, 8), :] = total


def pick_matrix(kt, first, stride):
    parts = [kt.at[h][pl.ds(first, BLK, stride=stride), :] for h in range(2)]
    return jnp.concatenate(parts, axis=1)[:, :BLK].astype(BF16)


def self_energy_kernel(
    shifts,
    weights,
    green,
    neighbours,
    mats,
    out,
    low,
    high,
    halo,
    local,
    buf0,
    buf1,
    rec,
    snd,
    mid,
    idv,
    ids,
    crem,
    crv,
    qs,
    r1,
    r2,
    kt,
    mt,
    kr,
    sst,
    sig,
    held,
    wide,
    sorted_mats,
    codes,
    hs,
    ls,
    zs,
    zr,
    rs,
    rr,
    fs,
    fr,
    cs,
    cr,
    ps,
    pr,
):
    me = lax.axis_index("atom")
    energy = lax.axis_index("energy")
    z, x, y = me // 16, (me // 4) % 4, me % 4
    buf = (buf0, buf1)

    def device(dz, dx, dy):
        return {"atom": (z + dz) * 16 + ((x + dx) % 4) * 4 + (y + dy) % 4}

    def remote(src, dst, send, recv, to):
        return pltpu.make_async_remote_copy(
            src_ref=src,
            dst_ref=dst,
            send_sem=send,
            recv_sem=recv,
            device_id=to,
            device_id_type=pl.DeviceIdType.MESH,
        )

    ring = (x, y)
    ring_to = (lambda d: device(0, d, 0), lambda d: device(0, 0, d))
    last = (y, x)
    last_to = (ring_to[1], ring_to[0])
    down, up = device(-1, 0, 0), device(1, 0, 0)

    barrier = pltpu.get_barrier_semaphore()

    @pl.when(energy > 0)
    def _():
        pl.semaphore_signal(
            barrier, inc=1, device_id={"energy": energy - 1}, device_id_type=pl.DeviceIdType.MESH
        )

    @pl.when(energy < 3)
    def _():
        pl.semaphore_signal(
            barrier, inc=1, device_id={"energy": energy + 1}, device_id_type=pl.DeviceIdType.MESH
        )

    for to in (ring_to[0](1), ring_to[0](-1), ring_to[1](1), ring_to[1](-1)):
        pl.semaphore_signal(barrier, inc=1, device_id=to, device_id_type=pl.DeviceIdType.MESH)

    @pl.when(z > 0)
    def _():
        pl.semaphore_signal(barrier, inc=1, device_id=down, device_id_type=pl.DeviceIdType.MESH)

    @pl.when(z < 3)
    def _():
        pl.semaphore_signal(barrier, inc=1, device_id=up, device_id_type=pl.DeviceIdType.MESH)

    wide[...] = green[...].astype(F32)
    real = wide[pl.ds(0, ATOMS * BLK, stride=2), :]
    imag = wide[pl.ds(1, ATOMS * BLK, stride=2), :]
    left = lax.broadcasted_iota(jnp.int32, real.shape, 1) < HALF
    low[...] = jnp.where(left, real, pltpu.roll(imag, HALF, 1)).astype(BF16)
    high[...] = jnp.where(left, pltpu.roll(real, HALF, 1), imag).astype(BF16)
    lower_block = convolve(low[...], high[...], lag_bands(shifts, weights))
    local[0] = lower_block
    buf0[pl.ds((x * 4 + z) * 4, 4)] = lower_block

    lists, key, where = make_lists(neighbours[...], me)
    codes[...] = lists

    kd = ENTRIES * DIRS
    to = lax.broadcasted_iota(jnp.int32, (kd, kd), 0)
    at = lax.broadcasted_iota(jnp.int32, (kd, kd), 1)
    order = jnp.zeros((kd, kd), jnp.bool_)
    for d in range(DIRS):
        order = order | ((to >= ENTRIES * d) & (to < ENTRIES * (d + 1)) & (at == (to - ENTRIES * d) * DIRS + d))
    sorted_mats[...] = dot(order.astype(F32).astype(BF16), mats[...]).astype(BF16)
    row = lax.broadcasted_iota(jnp.int32, (16, ENTRIES), 0)
    choice = (row == jnp.broadcast_to(key, row.shape)).astype(F32).astype(BF16)
    for d in range(DIRS):
        crem[pl.ds(16 * d, 16), :] = dot(choice, sorted_mats[pl.ds(ENTRIES * d, ENTRIES), :]).astype(BF16)
    spreaders(qs)
    expand(sorted_mats[...], qs, r1, r2)
    pl.semaphore_wait(barrier, 8 - z // 3 - (3 - z) // 3 - energy // 3 - (3 - energy) // 3)

    def lower():
        return remote(low, halo, hs.at[0], hs.at[1], {"energy": energy - 1})

    @pl.when(energy > 0)
    def _():
        lower().start()

    @pl.when(energy == 3)
    def _():
        halo[...] = jnp.zeros_like(halo)

    def place(p, r, s, h):
        return buf[p].at[pl.ds((r * 4 + s) * 4 + 2 * h, 2)]

    def ask(p, i, src, codes_src, slot, to):
        return [
            remote(codes_src, idv.at[p, slot], cs.at[p, i], cr.at[p, i], to),
            remote(src, crv.at[p, slot], ps.at[p, i], pr.at[p, i], to),
        ]

    def climb(p, k, s, h):
        spot = place(p, ring[p], s, h)
        return remote(spot, spot, zs.at[p, 0, k, h], zr.at[p, 0, k, h], up)

    def descend(p, k, s, h):
        spot = place(p, ring[p], s, h)
        return remote(spot, spot, zs.at[p, 1, k, h], zr.at[p, 1, k, h], down)

    def around(p, i, s, h):
        spot = place(p, ring[p], s, h)
        return remote(spot, spot, rs.at[p, i, s, h], rr.at[p, i, s, h], ring_to[p](1 - 2 * i))

    def onward(p, s, h):
        spot = place(p, (ring[p] + (3, 1)[h]) % 4, s, h)
        return remote(spot, spot, rs.at[p, 2, s, h], rr.at[p, 2, s, h], ring_to[p](1 - 2 * h))

    def deliver(p, s, h):
        around(p, h, s, h).start()
        around(p, 1 - h, s, h).start()

    def arrived(p, r, s, i, h):
        spot = place(p, r, s, h)
        remote(spot, spot, rs.at[p, i, s, h], rr.at[p, i, s, h], ring_to[p](1)).wait_recv()

    def relay(p, s):
        for h in range(2):
            arrived(p, (ring[p] + (3, 1)[h]) % 4, s, h, h)
            onward(p, s, h).start()

    def begin(p):
        if p == 1:
            c = pltpu.make_async_copy(local.at[p], buf[p].at[pl.ds((ring[p] * 4 + z) * 4, 4)], ls.at[p])
            c.start()
            c.wait()
        for h in range(2):

            @pl.when(z < 3)
            def _():
                climb(p, 0, z, h).start()

            @pl.when(z > 0)
            def _():
                descend(p, 0, z, h).start()

            deliver(p, z, h)

    def lower_arrived():
        remote(low, halo, hs.at[0], hs.at[1], {"energy": energy + 1}).wait_recv()

    def begin_upper():
        local[1] = convolve(high[...], halo[...], lag_bands(shifts, weights))
        begin(1)

    begin(0)
    sent = []
    for p in range(2):
        for i, d in enumerate((1, -1)):
            for c in ask(p, i, crem, codes, last[p], last_to[p](d)):
                c.start()
                sent.append(c)
    own_codes = [pltpu.make_async_copy(codes, ids.at[p, last[p]], ls.at[2 + p]) for p in range(2)]
    for c in own_codes:
        c.start()

    def local_products(n):
        products(ENTRIES, r1, r2, kt, 3 * n, 3 * n + 3)

    def local_sums(n):
        to = lax.broadcasted_iota(jnp.int32, (ATOMS * ATOMS, ENTRIES), 0)
        spread = (to == jnp.broadcast_to(where, to.shape)).astype(F32).astype(BF16)

        @pl.loop(36 * n, 36 * n + 36, step=12)
        def _(r):
            for u in range(12):
                at = pl.multiple_of((r + u) * ENTRIES, 8)
                both = jnp.concatenate([kt[h, pl.ds(at, ENTRIES), :] for h in range(2)], axis=1)
                summed = dot(spread, both.astype(BF16))
                for h in range(2):
                    mt[h, pl.ds((r + u) * 17, 16), :] = summed[:, SPAN * h : SPAN * (h + 1)]

    def local_energy():
        for a in range(ATOMS):
            acc = [jnp.zeros((BLK, SPAN), F32)] * 2
            for n in range(ATOMS):
                m = pick_matrix(mt, a * ATOMS + n, 17)
                for p in range(2):
                    acc[p] = acc[p] + dot(m, local[p, n])
            for p in range(2):
                sig[p, a] = acc[p]

    def forward_lists():
        for p in range(2):
            slot = (last[p] + 3) % 4
            for c in ask(p, 0, crem, codes, slot, last_to[p](-1)):
                c.wait_recv()
            for c in ask(p, 2, crv.at[p, slot], idv.at[p, slot], slot, last_to[p](1)):
                c.start()
                sent.append(c)

    def take_lists():
        moved = []
        for p in range(2):
            for i, j in ((1, 1), (2, 2)):
                slot = (last[p] + j) % 4
                for c in ask(p, i, crv.at[p, slot], idv.at[p, slot], slot, last_to[p](1)):
                    c.wait_recv()
            for j in range(1, 4):
                slot = (last[p] + j) % 4
                c = pltpu.make_async_copy(idv.at[p, slot], ids.at[p, slot], ls.at[4 + 3 * p + j - 1])
                c.start()
                moved.append(c)
        for c in own_codes + moved:
            c.wait()

    def remote_expand():
        sets = [crem[...]] + [crv[p, (last[p] + j) % 4] for p in range(2) for j in range(1, 4)]
        xs = jnp.concatenate([v[16 * d : 16 * (d + 1)] for d in range(DIRS) for v in sets], axis=0)
        expand(xs, qs, r1, r2)

    def remote_products(n):
        products(7 * 16, r1, r2, kt, (0, 5, 10)[n], (5, 10, 14)[n], 7 * 16 + 1)

    def remote_matrices(n):
        @pl.loop(14 * n, 14 * n + 14, step=7)
        def _(e):
            for u in range(7):
                kr[e + u] = pick_matrix(kt, (e + u) // REMOTE * 16 + (e + u) % REMOTE, 7 * 16 + 1)

    def rise(p, k):
        for h in range(2):

            @pl.when(z - 1 - k >= 0)
            def _():
                s = z - 1 - k
                spot = place(p, ring[p], s, h)
                remote(spot, spot, zs.at[p, 0, k, h], zr.at[p, 0, k, h], down).wait_recv()
                if k < 2:

                    @pl.when(z < 3)
                    def _():
                        climb(p, k + 1, s, h).start()

                deliver(p, s, h)

            @pl.when(z + 1 + k <= 3)
            def _():
                s = z + 1 + k
                spot = place(p, ring[p], s, h)
                remote(spot, spot, zs.at[p, 1, k, h], zr.at[p, 1, k, h], up).wait_recv()
                if k < 2:

                    @pl.when(z > 0)
                    def _():
                        descend(p, k + 1, s, h).start()

                deliver(p, s, h)

    def pass_on(p, k):
        if k == 0:
            relay(p, z)
        else:

            @pl.when(z - k >= 0)
            def _():
                relay(p, z - k)

            @pl.when(z + k <= 3)
            def _():
                relay(p, z + k)

    @pl.when((energy == 0) | (energy == 2))
    def _():
        lower_arrived()
        begin_upper()

    @pl.when(energy == 3)
    def _():
        begin_upper()

    forward_lists()
    local_products(0)
    rise(0, 0)
    local_products(1)
    pass_on(0, 0)
    local_products(2)

    @pl.when(energy == 1)
    def _():
        lower_arrived()
        begin_upper()

    local_products(3)
    rise(1, 0)
    local_sums(0)
    rise(0, 1)
    local_sums(1)
    pass_on(1, 0)
    local_sums(2)
    pass_on(0, 1)
    local_sums(3)
    rise(1, 1)
    take_lists()
    remote_expand()
    rise(0, 2)
    remote_products(0)
    pass_on(1, 1)
    remote_products(1)
    pass_on(0, 2)
    rise(1, 2)
    remote_products(2)
    pass_on(0, 3)
    remote_matrices(0)
    pass_on(1, 2)
    for n in range(1, 4):
        remote_matrices(n)
    pass_on(1, 3)
    for n in range(4, 6):
        remote_matrices(n)

    for p in range(2):
        buf[p][64] = jnp.zeros((BLK, SPAN), BF16)

    def contribution(p, j):
        slot = (last[p] + j) % 4
        q = 0 if j == 0 else 3 * p + j
        running = None
        for t in range(REMOTE):
            source = jnp.where(ids[p, slot, 2 + p, t] == last[p], ids[p, slot, p, t], 64)
            term = dot(kr[q * REMOTE + t], buf[p][source])
            same = ids[p, slot, 4, t] == ids[p, slot, 4, max(t - 1, 0)]
            running = term if running is None else jnp.where(same, 1.0, 0.0) * running + term
            sst[t] = running
        atoms = [ids[p, slot, 4, t] for t in range(REMOTE)]
        parts = []
        for a in range(ATOMS):
            upto = sum(jnp.where(v <= a, 1, 0) for v in atoms)
            last_one = jnp.maximum(upto - 1, 0)
            some = jnp.where((upto > 0) & (ids[p, slot, 4, last_one] == a), 1.0, 0.0)
            parts.append(sst[last_one] * some)
        return parts

    def offer(p, j):
        for a, v in enumerate(contribution(p, j)):
            snd[p, j, a] = v.astype(BF16)

    half = ATOMS // 2
    top = (pl.ds(0, half), pl.ds(half, half))

    def send(p, i, n, src, dst):
        c = remote(src, dst, fs.at[p, i, n], fr.at[p, i, n], last_to[p](1 - 2 * i))
        c.start()
        sent.append(c)

    def taken(p, i, n, spot):
        remote(spot, spot, fs.at[p, i, n], fr.at[p, i, n], last_to[p](1)).wait_recv()

    for p in range(2):
        for s in range(4):
            for h in range(2):
                arrived(p, (ring[p] + (1, 3)[h]) % 4, s, 1 - h, h)
                arrived(p, (ring[p] + 2) % 4, s, 2, h)
        offer(p, 2)
        for i in range(2):
            send(p, i, 0, snd.at[p, 2, top[i]], mid.at[p, i])
        for i, j in enumerate((1, 3)):
            parts = contribution(p, j)
            for a in range(half * (1 - i), half * (2 - i)):
                snd[p, j, a] = parts[a].astype(BF16)
            send(p, i, 1, snd.at[p, j, top[1 - i]], rec.at[p, i, top[1 - i]])
            for a in range(half):
                held[p, i, a] = parts[half * i + a]
    local_energy()
    for p in range(2):
        for a, v in enumerate(contribution(p, 0)):
            sig[p, a] += v
        for i, j in enumerate((1, 3)):
            taken(p, i, 0, mid.at[p, i])
            for a in range(half):
                snd[p, j, half * i + a] = (held[p, i, a] + mid[p, i, a].astype(F32)).astype(BF16)
            send(p, i, 2, snd.at[p, j, top[i]], rec.at[p, i, top[i]])
    for p in range(2):
        for i in range(2):
            taken(p, i, 1, rec.at[p, i, top[1 - i]])
            taken(p, i, 2, rec.at[p, i, top[i]])
        for a in range(ATOMS):
            sig[p, a] += rec[p, 0, a].astype(F32) + rec[p, 1, a].astype(F32)
    left = lax.broadcasted_iota(jnp.int32, (BLK, SPAN), 1) < HALF
    for a in range(ATOMS):
        lower_half, upper_half = sig[0, a], sig[1, a]
        out[pl.ds(a * 2 * BLK, BLK, stride=2), :] = jnp.where(left, lower_half, pltpu.roll(upper_half, HALF, 1))
        out[pl.ds(a * 2 * BLK + 1, BLK, stride=2), :] = jnp.where(left, pltpu.roll(lower_half, HALF, 1), upper_half)

    @pl.when(energy > 0)
    def _():
        lower().wait_send()

    for c in sent:
        c.wait_send()
    for p in range(2):
        for k in range(3):

            @pl.when((z < 3) & (z - k >= 0))
            def _():
                for h in range(2):
                    climb(p, k, z - k, h).wait_send()

            @pl.when((z > 0) & (z + k <= 3))
            def _():
                for h in range(2):
                    descend(p, k, z + k, h).wait_send()

        for s in range(4):
            for h in range(2):
                around(p, 0, s, h).wait_send()
                around(p, 1, s, h).wait_send()
                onward(p, s, h).wait_send()


def self_energy(shifts, weights, green, neighbours, mats):
    smem = pl.BlockSpec(memory_space=pltpu.SMEM)
    vmem = pl.BlockSpec(memory_space=pltpu.VMEM)
    dma = pltpu.SemaphoreType.DMA
    block = (BLK, SPAN)
    rows = DIRS * 7 * 16
    return pl.pallas_call(
        self_energy_kernel,
        out_shape=jax.ShapeDtypeStruct((2 * ATOMS * BLK, SPAN), F32),
        in_specs=[smem] * 2 + [vmem] * 3,
        out_specs=vmem,
        scratch_shapes=[
            pltpu.VMEM((ATOMS * BLK, SPAN), BF16),
            pltpu.VMEM((ATOMS * BLK, SPAN), BF16),
            pltpu.VMEM((ATOMS * BLK, SPAN), BF16),
            pltpu.VMEM((2, ATOMS) + block, BF16),
            pltpu.VMEM((65,) + block, BF16),
            pltpu.VMEM((65,) + block, BF16),
            pltpu.VMEM((2, 2, ATOMS) + block, BF16),
            pltpu.VMEM((2, 4, ATOMS) + block, BF16),
            pltpu.VMEM((2, 2, ATOMS // 2) + block, BF16),
            pltpu.VMEM((2, 4, 8, SPAN), jnp.int32),
            pltpu.SMEM((2, 4, 8, SPAN), jnp.int32),
            pltpu.VMEM((DIRS * 16, BLK), BF16),
            pltpu.VMEM((2, 4, DIRS * 16, BLK), BF16),
            pltpu.VMEM((2 * ORB, BLK, 2 * SPAN), BF16),
            pltpu.VMEM((ORB, rows, 2 * SPAN), F32),
            pltpu.VMEM((ORB, rows, 2 * SPAN), F32),
            pltpu.VMEM((2, BLK * (7 * 16 + 1), SPAN), F32),
            pltpu.VMEM((2, BLK * 17, SPAN), F32),
            pltpu.VMEM((7 * REMOTE, BLK, BLK), BF16),
            pltpu.VMEM((REMOTE,) + block, F32),
            pltpu.VMEM((2, ATOMS) + block, F32),
            pltpu.VMEM((2, 2, ATOMS // 2) + block, F32),
            pltpu.VMEM((2 * ATOMS * BLK, SPAN), F32),
            pltpu.VMEM((ENTRIES * DIRS, BLK), BF16),
            pltpu.VMEM((8, SPAN), jnp.int32),
            dma((2,)),
            dma((10,)),
            dma((2, 2, 3, 2)),
            dma((2, 2, 3, 2)),
            dma((2, 3, 4, 2)),
            dma((2, 3, 4, 2)),
            dma((2, 2, 3)),
            dma((2, 2, 3)),
            dma((2, 3)),
            dma((2, 3)),
            dma((2, 3)),
            dma((2, 3)),
        ],
        compiler_params=pltpu.CompilerParams(
            collective_id=0, has_side_effects=True, vmem_limit_bytes=60 * 1024 * 1024
        ),
        name="self_energy",
    )(shifts, weights, green, neighbours, mats)


def rows_of(blocks):
    return blocks.transpose(0, 2, 3, 1, 4).reshape(2 * ATOMS * BLK, blocks.shape[-1])


def on_device(green, coupling, neighbours, shifts, weights):
    mats = coupling.reshape(ENTRIES * DIRS, BLK)
    out = self_energy(shifts, weights, rows_of(green), neighbours, mats).astype(BF16)
    return out.reshape(ATOMS, ORB, ORB, 2, SPAN).transpose(0, 3, 1, 2, 4)


def solution(mesh):
    placed = (P("atom", None, None, None, "energy"), P("atom", None), P("atom", None), P(), P())
    return jax.shard_map(
        on_device,
        mesh=mesh,
        in_specs=placed,
        out_specs=P("atom", None, None, None, "energy"),
        check_vma=False,
    )
```
